32 devices in a mesh: sea: 8 (over y, x, core), fault: 4 (over z).
Axes of the slice: x: 2, y: 2, z: 4, core: 2. Of those that a mesh axis runs over, the one named last changes fastest.
Arguments:
- slip_rate: bfloat16 [16384, 128], P(('fault', 'sea')), may hold values from -6 to 6
- near_blocks: bfloat16 [8, 4, 8, 256, 256], P('sea', 'fault'), may hold values from -0.375 to 0.375
- near_rows: int32 [8, 4, 8], P('sea', 'fault'), may hold values from 0 to 3
- near_cols: int32 [8, 4, 8], P('sea', 'fault'), may hold values from 0 to 15
- near_scale: float32 [8, 4, 8], P('sea', 'fault'), may hold values from 0.1 to 0.5
- far_left: bfloat16 [8, 4, 24, 48, 256], P('sea', 'fault'), may hold values from -0.875 to 0.875
- far_right: bfloat16 [8, 4, 24, 48, 256], P('sea', 'fault'), may hold values from -0.375 to 0.375
- far_rows: int32 [8, 4, 24], P('sea', 'fault'), may hold values from 0 to 3
- far_cols: int32 [8, 4, 24], P('sea', 'fault'), may hold values from 0 to 15
- far_rank: int32 [8, 4, 24], P('sea', 'fault'), may hold values from 16 to 48, as said below
- far_scale: float32 [8, 4, 24], P('sea', 'fault'), may hold values from 0.1 to 0.5
- sea_depth: float32 [128, 64], P('sea', 'fault'), may hold values from 0.3 to 1
- wet_mask: int32 [128, 64], P('sea', 'fault'), may hold values 0 or 1
Outputs:
- uplift: float32 [128, 64, 128], P('sea', 'fault')
- sea_level: float32 [128, 64, 128], P('sea', 'fault')
The draws below stay inside these ranges and needn't reach their ends.
Inputs may be any that keep to these rules, and one draw needn't show every extreme that they name: `far_rank`: block 0 of every device has rank 48; every rank is at least 16.
All inputs are finite; a program needn't handle non-finite values. No bound on the sum of `wet_mask` on one device may be relied on, other than what follows from the above.
Results may differ from the reference program's by a relative error of at most 0.0024.
Values may be sent and summed in bfloat16 or wider, within the bound.
No kernel may reach another device: no remote copies, remote signals or barrier semaphores. Data moves between devices by JAX's collectives and lax.ppermute only.
A program may use at most 64 MiB of HBM per device.

```python
import math
import jax
import jax.numpy as jnp
from jax import lax

LEAF = 256
RANK = 48
SCENARIOS = 128
BY = 16
COL_LEAVES = 16
NEAR = 8
FAR = 24
STEPS = 6
ROW_LEAVES = 4
ELEMENTS = 16384
GRID_Y = 128
GRID_X = 64
N_SEA = 8
N_FAULT = 4


def draw_far_rank(key, part):
    drawn_ranks = jax.random.randint(key, (N_SEA, N_FAULT, FAR), RANK // 3, RANK + 1)
    return drawn_ranks.at[:, :, 0].set(RANK).astype(jnp.int32)


def plant(entries, stream_key, least, largest):
    dims = entries.shape
    index_at = [jax.random.randint(jax.random.fold_in(stream_key, axis), (), 0, dims[axis]) for axis in range(len(dims))]
    entries = entries.at[tuple(index_at)].set(least)
    longest = dims.index(max(dims))
    index_at[longest] = (index_at[longest] + 1) % dims[longest]
    return entries.at[tuple(index_at)].set(largest)


def block_levels(stream_key, dims, pieces, low, top_value):
    def one(dim, blocks):
        heights = jax.random.uniform(jax.random.fold_in(jax.random.fold_in(stream_key, 6), dim), (blocks,), jnp.float32, low / len(pieces), top_value / len(pieces))
        return jnp.repeat(jnp.exp(heights), dims[dim] // blocks).reshape((-1,) + (1,) * (len(dims) - dim - 1))

    gain = one(*pieces[0])
    for cut in pieces[1:]:
        gain = gain * one(*cut)
    return gain


def noise(rng, extent, scale, most, pieces=(), dtype=jnp.bfloat16):
    entries = scale * jax.random.normal(rng, extent, jnp.float32)
    if pieces:
        entries = entries * block_levels(rng, extent, pieces, -0.22, 0.18)
    return jnp.clip(entries, -most, most).astype(dtype)


def setup_inputs(seed: int = 0) -> dict:
    arg_keys = jax.random.split(jax.random.key(seed), 14)
    slip_rate = noise(arg_keys[0], (ELEMENTS, SCENARIOS), 1.0, 6.0, ((0, 32),))
    near_blocks = noise(arg_keys[1], (N_SEA, N_FAULT, NEAR, LEAF, LEAF), LEAF ** -0.5, 0.375, ((0, 8), (1, 4)))
    near_rows = plant(jax.random.randint(arg_keys[2], (N_SEA, N_FAULT, NEAR), 0, ROW_LEAVES), jax.random.fold_in(arg_keys[2], 1), 0, ROW_LEAVES - 1).astype(jnp.int32)
    near_cols = plant(jax.random.randint(arg_keys[3], (N_SEA, N_FAULT, NEAR), 0, COL_LEAVES), jax.random.fold_in(arg_keys[3], 1), 0, COL_LEAVES - 1).astype(jnp.int32)
    near_scale = jnp.clip(jnp.exp(math.log(0.5) - 1.609438 * jax.random.uniform(arg_keys[4], (N_SEA, N_FAULT, NEAR), jnp.float32) ** block_levels(arg_keys[4], (N_SEA, N_FAULT, NEAR), ((0, 8), (1, 4)), -0.2, 0.2)), 0.1, 0.5)
    far_left = noise(arg_keys[5], (N_SEA, N_FAULT, FAR, RANK, LEAF), RANK ** -0.5, 0.875, ((0, 8), (1, 4)))
    far_right = noise(arg_keys[6], (N_SEA, N_FAULT, FAR, RANK, LEAF), LEAF ** -0.5, 0.375, ((0, 8), (1, 4)))
    far_rows = plant(jax.random.randint(arg_keys[7], (N_SEA, N_FAULT, FAR), 0, ROW_LEAVES), jax.random.fold_in(arg_keys[7], 1), 0, ROW_LEAVES - 1).astype(jnp.int32)
    far_cols = plant(jax.random.randint(arg_keys[8], (N_SEA, N_FAULT, FAR), 0, COL_LEAVES), jax.random.fold_in(arg_keys[8], 1), 0, COL_LEAVES - 1).astype(jnp.int32)
    far_rank = draw_far_rank(jax.random.fold_in(arg_keys[13], 71), 0)
    far_scale = jnp.clip(jnp.exp(math.log(0.5) - 1.609438 * jax.random.uniform(arg_keys[10], (N_SEA, N_FAULT, FAR), jnp.float32) ** block_levels(arg_keys[10], (N_SEA, N_FAULT, FAR), ((0, 8), (1, 4)), -0.2, 0.2)), 0.1, 0.5)
    sea_depth = jnp.clip(0.3 + 0.7 * jax.random.uniform(arg_keys[11], (GRID_Y, GRID_X), jnp.float32) ** block_levels(arg_keys[11], (GRID_Y, GRID_X), ((0, 8), (1, 4)), -0.2, 0.2), 0.3, 1.0)
    wet_mask = plant((jax.random.randint(arg_keys[12], (GRID_Y, GRID_X), 0, 5) < 4).astype(jnp.int32), jax.random.fold_in(arg_keys[12], 1), 0, 1)
    return dict(slip_rate=slip_rate, near_blocks=near_blocks, near_rows=near_rows, near_cols=near_cols, near_scale=near_scale, far_left=far_left, far_right=far_right, far_rows=far_rows, far_cols=far_cols, far_rank=far_rank, far_scale=far_scale, sea_depth=sea_depth, wet_mask=wet_mask)


gravity_step = 0.7
height_step = 0.7


def advance(height, east_flow, north_flow, depth_pad):
    new_east = east_flow[1:-1, :-1] - gravity_step * (height[1:-1, 1:] - height[1:-1, :-1])
    east_depth = jnp.minimum(depth_pad[1:-1, :-1], depth_pad[1:-1, 1:])
    flux_east = east_depth[:, :, None] * new_east
    new_north = north_flow[:-1, 1:-1] - gravity_step * (height[1:, 1:-1] - height[:-1, 1:-1])
    north_depth = jnp.minimum(depth_pad[:-1, 1:-1], depth_pad[1:, 1:-1])
    flux_north = north_depth[:, :, None] * new_north
    change = flux_east[:, 1:] - flux_east[:, :-1] + flux_north[1:] - flux_north[:-1]
    new_height = height[1:-1, 1:-1] - height_step * change
    return new_height, new_east[:, 1:], new_north[1:]


def cluster_uplift(inputs, leaves):
    near_blocks, near_rows, near_cols, near_scale, far_left, far_right, far_rows, far_cols, far_rank, far_scale = inputs
    fault_index = jnp.arange(N_FAULT)[:, None]
    targets = jnp.arange(ROW_LEAVES)
    near_slip = leaves[fault_index, near_cols]
    near_term = jnp.einsum('fbij,fbjs->fbis', near_blocks.astype(jnp.float32), near_slip.astype(jnp.float32))
    near_weight = (near_rows[..., None] == targets).astype(jnp.float32) * near_scale[..., None]
    total = jnp.einsum('fbr,fbis->ris', near_weight, near_term, precision=lax.Precision.HIGHEST)
    far_slip = leaves[fault_index, far_cols]
    coeffs = jnp.einsum('fbkc,fbcs->fbks', far_right.astype(jnp.float32), far_slip.astype(jnp.float32))
    kept = jnp.arange(RANK)[:, None] < far_rank[..., None, None]
    coeffs = jnp.where(kept, coeffs, jnp.float32(0.0)).astype(jnp.bfloat16)
    far_term = jnp.einsum('fbki,fbks->fbis', far_left.astype(jnp.float32), coeffs.astype(jnp.float32))
    far_weight = (far_rows[..., None] == targets).astype(jnp.float32) * far_scale[..., None]
    total = total + jnp.einsum('fbr,fbis->ris', far_weight, far_term, precision=lax.Precision.HIGHEST)
    return total.reshape(BY, GRID_X, SCENARIOS)


def reference(slip_rate, near_blocks, near_rows, near_cols, near_scale, far_left, far_right, far_rows, far_cols, far_rank, far_scale, sea_depth, wet_mask):
    leaves = slip_rate.reshape(N_FAULT, COL_LEAVES, LEAF, SCENARIOS)
    inputs = (near_blocks, near_rows, near_cols, near_scale, far_left, far_right, far_rows, far_cols, far_rank, far_scale)
    stacked = lax.map(lambda entry: cluster_uplift(entry, leaves), inputs)
    uplift = stacked.reshape(GRID_Y, GRID_X, SCENARIOS)
    wet = wet_mask.astype(jnp.float32)
    depth_pad = jnp.pad(sea_depth * wet, 1)
    height = uplift * wet[:, :, None]
    east_flow = jnp.zeros_like(height)
    north_flow = jnp.zeros_like(height)
    margin = ((1, 1), (1, 1), (0, 0))
    for step_index in range(STEPS):
        height, east_flow, north_flow = advance(jnp.pad(height, margin), jnp.pad(east_flow, margin), jnp.pad(north_flow, margin), depth_pad)
    return uplift, height
```

```python
import functools

import jax
import jax.numpy as jnp
from jax import lax
from jax.experimental import pallas as pl
from jax.experimental.pallas import tpu as pltpu
from jax.sharding import PartitionSpec as P

STEPS = 6
SUB = 8
TILE = 16
LANES = 128

gravity_step = 0.7
height_step = 0.7


def swap(x, axis, k):
    count = lax.axis_size(axis)
    return lax.ppermute(x, axis, [(i, i ^ k) for i in range(count)])


def pieces(d, gap):
    hi = d.astype(jnp.bfloat16).astype(jnp.float32)
    rest = d - hi
    mid = rest.astype(jnp.bfloat16).astype(jnp.float32)
    low = rest - mid
    packed = hi + pltpu.roll(mid, gap, 1) + pltpu.roll(low, 2 * gap, 1)
    return packed.astype(jnp.bfloat16)


def joined(tile, gap):
    t = tile.astype(jnp.float32)
    lanes = t.shape[1]
    d = (t + pltpu.roll(t, lanes - gap, 1)) + pltpu.roll(t, lanes - 2 * gap, 1)
    lane = lax.broadcasted_iota(jnp.int32, t.shape, 1)
    return jnp.where(lane < gap, d, 0.0)


def blocks_kernel(dims, *refs):
    n_sea, n_fault, n_near, n_far, leaf, rank, rows, leaf_count, bx, wx = dims
    ints, scales, tile = refs[:3]
    slots = refs[3 : 3 + n_sea]
    near, left, right = refs[3 + n_sea : 6 + n_sea]
    own = refs[6 + n_sea]
    outs = refs[7 + n_sea : 6 + n_sea + n_fault]
    slip, near_v, left_v, right_v, coeffs, acc, wide, sems = refs[6 + n_sea + n_fault :]
    sea = ints[0]
    fault = ints[1]
    members = slip.shape[1]
    by = tile.shape[0]
    width = leaf_count * leaf // by
    halo = (wx - bx) // 2
    copies = []
    for k in range(n_sea):
        start = pl.multiple_of((sea ^ k) * rows, rows)
        copies.append(pltpu.make_async_copy(slots[k], slip.at[pl.ds(start, rows)], sems.at[k]))
    loads = [
        pltpu.make_async_copy(right, right_v, sems.at[n_sea]),
        pltpu.make_async_copy(near, near_v, sems.at[n_sea + 1]),
        pltpu.make_async_copy(left, left_v, sems.at[n_sea + 2]),
    ]
    for copy in copies + loads:
        copy.start()
    acc[...] = jnp.zeros_like(acc)
    edge = jnp.zeros((halo,) + wide.shape[1:], jnp.float32)
    wide[0:halo] = edge
    wide[halo + width :] = edge
    for copy in copies:
        copy.wait()
    at_near_rows, at_near_cols = 2, 2 + n_near
    at_far_rows = 2 + 2 * n_near
    at_far_cols, at_far_rank = at_far_rows + n_far, at_far_rows + 2 * n_far
    loads[0].wait()
    level = lax.broadcasted_iota(jnp.int32, (rank, members), 0)
    for b in range(n_far):
        start = pl.multiple_of(ints[at_far_cols + b] * leaf, leaf)
        c = jnp.dot(
            right_v[b], slip[pl.ds(start, leaf), :], preferred_element_type=jnp.float32
        )
        coeffs[b] = jnp.where(level < ints[at_far_rank + b], c, 0.0).astype(jnp.bfloat16)
    loads[1].wait()
    for b in range(n_near):
        start = pl.multiple_of(ints[at_near_cols + b] * leaf, leaf)
        target = pl.multiple_of(ints[at_near_rows + b] * leaf, leaf)
        term = jnp.dot(
            near_v[b], slip[pl.ds(start, leaf), :], preferred_element_type=jnp.float32
        )
        acc[pl.ds(target, leaf), :] += scales[b] * term
    loads[2].wait()
    for b in range(n_far):
        target = pl.multiple_of(ints[at_far_rows + b] * leaf, leaf)
        term = lax.dot_general(
            left_v[b], coeffs[b], (((0,), (0,)), ((), ())), preferred_element_type=jnp.float32
        )
        acc[pl.ds(target, leaf), :] += scales[n_near + b] * term
    for x in range(width):
        wide[halo + x] = acc[pl.ds(x, by, stride=width), :]
    own[...] = wide[pl.ds(fault * bx, wx)].reshape(wx * by, members)
    packed = pieces(tile[...], bx)
    for k in range(1, n_fault):
        part = wide[pl.ds((fault ^ k) * bx, wx)].reshape(wx * by, members)
        outs[k - 1][0 : wx * by] = part.astype(jnp.bfloat16)
        outs[k - 1][wx * by :] = packed


def sum_kernel(dims, *refs):
    n_fault, bx, wx, by = dims
    ints, tile, own = refs[:3]
    parts = refs[3 : 2 + n_fault]
    total, depth, uplift, near_edge, far_edge = refs[2 + n_fault :]
    sea = ints[0]
    fault = ints[1]
    halo = (wx - bx) // 2
    cells = wx * by
    s = own[...]
    for part in parts:
        s = s + part[0:cells].astype(jnp.float32)
    total[...] = s
    mid = tile[...]
    before = jnp.zeros_like(mid)
    after = jnp.zeros_like(mid)
    for k in range(1, n_fault):
        other = joined(parts[k - 1][cells:], bx)
        source = fault ^ k
        before = before + jnp.where(source == fault - 1, other, 0.0)
        after = after + jnp.where(source == fault + 1, other, 0.0)
    lanes = mid.shape[1]
    lane = lax.broadcasted_iota(jnp.int32, mid.shape, 1)
    d = jnp.where(lane < halo, pltpu.roll(before, lanes - (bx - halo), 1), 0.0)
    d = d + pltpu.roll(mid, halo, 1)
    d = d + pltpu.roll(jnp.where(lane < halo, after, 0.0), halo + bx, 1)
    depth[...] = d
    packed = pieces(d, lanes // 4)
    odd = sea & 1
    for y in range(by):
        uplift[y] = total[pl.ds(halo * by + y, bx, stride=by), :]
    stack = s.reshape(wx, by, s.shape[1])
    first = stack[:, 0:SUB, :].reshape(wx * SUB, -1).astype(jnp.bfloat16)
    last = stack[:, by - SUB :, :].reshape(wx * SUB, -1).astype(jnp.bfloat16)
    near_edge[0 : wx * SUB] = jnp.where(odd == 1, first, last)
    far_edge[0 : wx * SUB] = jnp.where(odd == 1, last, first)
    near_edge[wx * SUB :] = packed
    far_edge[wx * SUB :] = packed


def steps_kernel(dims, ints, total, depth, near_edge, far_edge, level, h, e, n, de, dn):
    bx, wx, by = dims
    halo = (wx - bx) // 2
    odd = ints[0] & 1
    span = by + 2 * SUB
    edge = wx * SUB
    lanes = depth.shape[1]
    near = near_edge[...].astype(jnp.float32)
    far = far_edge[...].astype(jnp.float32)
    prev = jnp.where(odd == 1, near, far)
    post = jnp.where(odd == 1, far, near)
    prev_d = joined(prev[edge:], lanes // 4)[by - SUB :]
    post_d = joined(post[edge:], lanes // 4)[0:SUB]
    d = jnp.concatenate([prev_d, depth[...], post_d], axis=0)
    east = jnp.minimum(d, pltpu.roll(d, lanes - 1, 1))
    north = jnp.minimum(d, pltpu.roll(d, span - 1, 0))
    wet = jnp.where(d > 0.0, 1.0, 0.0)
    zero = jnp.zeros((span, lanes), jnp.float32)
    for x in range(wx):
        column = jnp.concatenate(
            [prev[x * SUB : (x + 1) * SUB], total[x * by : (x + 1) * by], post[x * SUB : (x + 1) * SUB]],
            axis=0,
        )
        h[x] = column * jnp.broadcast_to(wet[:, x : x + 1], (span, lanes))
        de[x] = jnp.broadcast_to(east[:, x : x + 1], (span, lanes))
        dn[x] = jnp.broadcast_to(north[:, x : x + 1], (span, lanes))
        e[x] = zero
        n[x] = zero
    for step in range(STEPS):
        h_here = h[step]
        flux_before = None
        for x in range(step, wx - 1 - step):
            h_next = h[x + 1]
            new_east = e[x] - gravity_step * (h_next - h_here)
            e[x] = new_east
            flux = de[x] * new_east
            if flux_before is not None:
                new_north = n[x] - gravity_step * (pltpu.roll(h_here, span - 1, 0) - h_here)
                n[x] = new_north
                flux_north = dn[x] * new_north
                change = ((flux - flux_before) + flux_north) - pltpu.roll(flux_north, 1, 0)
                h[x] = h_here - height_step * change
            flux_before = flux
            h_here = h_next
    for y in range(by):
        level[y] = jnp.concatenate(
            [h[halo + x, SUB + y : SUB + y + 1, :] for x in range(bx)], axis=0
        )


def on_device(
    slip_rate,
    near_blocks,
    near_rows,
    near_cols,
    near_scale,
    far_left,
    far_right,
    far_rows,
    far_cols,
    far_rank,
    far_scale,
    sea_depth,
    wet_mask,
):
    by, bx = sea_depth.shape
    n_sea = lax.axis_size("sea")
    n_fault = lax.axis_size("fault")
    n_near = near_blocks.shape[2]
    n_far, rank, leaf = far_left.shape[2:]
    rows, members = slip_rate.shape
    leaf_count = by * bx * n_fault // leaf
    wx = bx + 2 * STEPS
    f32, bf16 = jnp.float32, jnp.bfloat16

    slots = [slip_rate]
    across = [swap(slip_rate, "sea", k) for k in range(2, n_sea, 2)]
    slots.append(swap(slip_rate, "sea", 1))
    for part in across:
        slots += [part, swap(part, "sea", 1)]

    place = jnp.stack([lax.axis_index("sea"), lax.axis_index("fault")]).astype(jnp.int32)
    ints = jnp.concatenate(
        [place]
        + [a.reshape(-1) for a in (near_rows, near_cols, far_rows, far_cols, far_rank)]
    )
    scales = jnp.concatenate([near_scale.reshape(-1), far_scale.reshape(-1)])
    tile = jnp.pad(sea_depth * wet_mask.astype(f32), ((0, 0), (0, LANES - bx)))

    anywhere = pl.BlockSpec(memory_space=pl.ANY)
    vector = pl.BlockSpec(memory_space=pltpu.VMEM)
    scalar = pl.BlockSpec(memory_space=pltpu.SMEM)
    cells = wx * by
    dims = (n_sea, n_fault, n_near, n_far, leaf, rank, rows, leaf_count, bx, wx)
    own, *chunks = pl.pallas_call(
        functools.partial(blocks_kernel, dims),
        out_shape=[jax.ShapeDtypeStruct((cells, members), f32)]
        + [jax.ShapeDtypeStruct((cells + by, members), bf16)] * (n_fault - 1),
        in_specs=[scalar, scalar, vector] + [anywhere] * (n_sea + 3),
        out_specs=[vector] * n_fault,
        scratch_shapes=[
            pltpu.VMEM((n_sea * rows, members), bf16),
            pltpu.VMEM(near_blocks.shape[2:], bf16),
            pltpu.VMEM(far_left.shape[2:], bf16),
            pltpu.VMEM(far_right.shape[2:], bf16),
            pltpu.VMEM((n_far, rank, members), bf16),
            pltpu.VMEM((leaf_count * leaf, members), f32),
            pltpu.VMEM((n_fault * bx + 2 * STEPS, by, members), f32),
            pltpu.SemaphoreType.DMA((n_sea + 3,)),
        ],
        name="blocks",
    )(ints, scales, tile, *slots, near_blocks[0, 0], far_left[0, 0], far_right[0, 0])

    got = [swap(chunks[k - 1], "fault", k) for k in range(1, n_fault)]

    edge = jax.ShapeDtypeStruct((wx * SUB + by, members), bf16)
    total, depth, uplift, near_edge, far_edge = pl.pallas_call(
        functools.partial(sum_kernel, (n_fault, bx, wx, by)),
        out_shape=[
            jax.ShapeDtypeStruct((cells, members), f32),
            jax.ShapeDtypeStruct((by, LANES), f32),
            jax.ShapeDtypeStruct((by, bx, members), f32),
            edge,
            edge,
        ],
        in_specs=[scalar] + [vector] * (1 + n_fault),
        out_specs=[vector] * 5,
        name="sums",
    )(ints, tile, own, *got)

    near_edge = swap(near_edge, "sea", 1)
    pairs = [(i, i + 1) for i in range(1, n_sea - 1, 2)]
    far_edge = lax.ppermute(far_edge, "sea", pairs + [(b, a) for a, b in pairs])

    span = by + 2 * SUB
    field = pltpu.VMEM((wx, span, members), f32)
    level = pl.pallas_call(
        functools.partial(steps_kernel, (bx, wx, by)),
        out_shape=jax.ShapeDtypeStruct((by, bx, members), f32),
        in_specs=[scalar] + [vector] * 4,
        out_specs=vector,
        scratch_shapes=[field] * 5,
        name="steps",
    )(ints, total, depth, near_edge, far_edge)
    return uplift, level


def solution(mesh):
    placed = (
        P(("fault", "sea"), None),
        P("sea", "fault", None, None, None),
        P("sea", "fault", None),
        P("sea", "fault", None),
        P("sea", "fault", None),
        P("sea", "fault", None, None, None),
        P("sea", "fault", None, None, None),
        P("sea", "fault", None),
        P("sea", "fault", None),
        P("sea", "fault", None),
        P("sea", "fault", None),
        P("sea", "fault"),
        P("sea", "fault"),
    )
    return jax.shard_map(
        on_device,
        mesh=mesh,
        in_specs=placed,
        out_specs=(P("sea", "fault", None), P("sea", "fault", None)),
        check_vma=False,
    )
```

```python
import functools

import jax
import jax.numpy as jnp
from jax import lax
from jax.experimental import pallas as pl
from jax.experimental.pallas import tpu as pltpu
from jax.sharding import PartitionSpec as P


STEPS = 6
SUB = 8
LANES = 128

gravity_step = 0.7
height_step = 0.7


def swap(x, axis, k):
    count = lax.axis_size(axis)
    return lax.ppermute(x, axis, [(i, i ^ k) for i in range(count)])


def pieces(d, gap):
    hi = d.astype(jnp.bfloat16).astype(jnp.float32)
    rest = d - hi
    mid = rest.astype(jnp.bfloat16).astype(jnp.float32)
    low = rest - mid
    packed = hi + pltpu.roll(mid, gap, 1) + pltpu.roll(low, 2 * gap, 1)
    return packed.astype(jnp.bfloat16)


def joined(tile, gap):
    t = tile.astype(jnp.float32)
    lanes = t.shape[1]
    d = (t + pltpu.roll(t, lanes - gap, 1)) + pltpu.roll(t, lanes - 2 * gap, 1)
    lane = lax.broadcasted_iota(jnp.int32, t.shape, 1)
    return jnp.where(lane < gap, d, 0.0)


def fetch_kernel(*refs):
    sources, refs = refs[:13], refs[13:]
    tables, scales, tile = refs[:3]
    targets, small, sems = refs[3:7], refs[7:16], refs[16]
    copies = [
        pltpu.make_async_copy(source, target, sems.at[k])
        for k, (source, target) in enumerate(zip(sources, small + targets))
    ]
    for copy in copies:
        copy.start()
    for copy in copies[:9]:
        copy.wait()
    near_rows, near_cols, near_scale, far_rows, far_cols, far_rank, far_scale = small[:7]
    for k, part in enumerate((near_rows, near_cols, far_rows, far_cols, far_rank)):
        tables[k : k + 1, 0 : part.shape[1]] = part[...]
    for k, part in enumerate((near_scale, far_scale)):
        scales[k : k + 1, 0 : part.shape[1]] = part[...]
    d = small[7][...] * small[8][...].astype(jnp.float32)
    by, bx = d.shape
    tile[...] = jnp.concatenate([d, jnp.zeros((by, LANES - bx), jnp.float32)], axis=1)
    for copy in copies[9:]:
        copy.wait()


def blocks_kernel(dims, *refs):
    n_sea, n_fault, n_near, n_far, leaf, rank, rows, leaf_count, bx, wx = dims
    tables, scales, tile = refs[:3]
    refs = refs[3:]
    slots = refs[:n_sea]
    near, left, right, own = refs[n_sea : 4 + n_sea]
    outs = refs[4 + n_sea : 3 + n_sea + n_fault]
    slip, coeffs, acc, wide = refs[3 + n_sea + n_fault :]
    sea = lax.axis_index("sea")
    fault = lax.axis_index("fault")
    members = slip.shape[1]
    by = tile.shape[0]
    width = leaf_count * leaf // by
    halo = (wx - bx) // 2
    for k in range(n_sea):
        start = pl.multiple_of((sea ^ k) * rows, rows)
        slip[pl.ds(start, rows)] = slots[k][...]
    acc[...] = jnp.zeros_like(acc)
    edge = jnp.zeros((halo,) + wide.shape[1:], jnp.float32)
    wide[0:halo] = edge
    wide[halo + width :] = edge
    level = lax.broadcasted_iota(jnp.int32, (rank, members), 0)
    for b in range(n_far):
        start = pl.multiple_of(tables[3, b] * leaf, leaf)
        c = jnp.dot(
            right[b], slip[pl.ds(start, leaf), :], preferred_element_type=jnp.float32
        )
        coeffs[b] = jnp.where(level < tables[4, b], c, 0.0).astype(jnp.bfloat16)
    for b in range(n_near):
        start = pl.multiple_of(tables[1, b] * leaf, leaf)
        target = pl.multiple_of(tables[0, b] * leaf, leaf)
        term = jnp.dot(
            near[b], slip[pl.ds(start, leaf), :], preferred_element_type=jnp.float32
        )
        acc[pl.ds(target, leaf), :] += scales[0, b] * term
    for b in range(n_far):
        target = pl.multiple_of(tables[2, b] * leaf, leaf)
        term = lax.dot_general(
            left[b], coeffs[b], (((0,), (0,)), ((), ())), preferred_element_type=jnp.float32
        )
        acc[pl.ds(target, leaf), :] += scales[1, b] * term
    for x in range(width):
        wide[halo + x] = acc[pl.ds(x, by, stride=width), :]
    own[...] = wide[pl.ds(fault * bx, wx)].reshape(wx * by, members)
    packed = pieces(tile[...], bx)
    for k in range(1, n_fault):
        part = wide[pl.ds((fault ^ k) * bx, wx)].reshape(wx * by, members)
        outs[k - 1][0 : wx * by] = part.astype(jnp.bfloat16)
        outs[k - 1][wx * by :] = packed


def sum_kernel(dims, *refs):
    n_fault, bx, wx, by = dims
    tile, own = refs[:2]
    parts = refs[2 : 1 + n_fault]
    total, depth, uplift, near_edge, far_edge = refs[1 + n_fault :]
    sea = lax.axis_index("sea")
    fault = lax.axis_index("fault")
    halo = (wx - bx) // 2
    cells = wx * by
    s = own[...]
    for part in parts:
        s = s + part[0:cells].astype(jnp.float32)
    total[...] = s
    mid = tile[...]
    before = jnp.zeros_like(mid)
    after = jnp.zeros_like(mid)
    for k in range(1, n_fault):
        other = joined(parts[k - 1][cells:], bx)
        source = fault ^ k
        before = before + jnp.where(source == fault - 1, other, 0.0)
        after = after + jnp.where(source == fault + 1, other, 0.0)
    lanes = mid.shape[1]
    lane = lax.broadcasted_iota(jnp.int32, mid.shape, 1)
    d = jnp.where(lane < halo, pltpu.roll(before, lanes - (bx - halo), 1), 0.0)
    d = d + pltpu.roll(mid, halo, 1)
    d = d + pltpu.roll(jnp.where(lane < halo, after, 0.0), halo + bx, 1)
    depth[...] = d
    packed = pieces(d, lanes // 4)
    odd = sea & 1
    for y in range(by):
        uplift[y] = total[pl.ds(halo * by + y, bx, stride=by), :]
    stack = s.reshape(wx, by, s.shape[1])
    first = stack[:, 0:SUB, :].reshape(wx * SUB, -1).astype(jnp.bfloat16)
    last = stack[:, by - SUB :, :].reshape(wx * SUB, -1).astype(jnp.bfloat16)
    near_edge[0 : wx * SUB] = jnp.where(odd == 1, first, last)
    far_edge[0 : wx * SUB] = jnp.where(odd == 1, last, first)
    near_edge[wx * SUB :] = packed
    far_edge[wx * SUB :] = packed


def steps_kernel(dims, total, depth, near_edge, far_edge, level, h, e, n, de, dn):
    bx, wx, by = dims
    halo = (wx - bx) // 2
    odd = lax.axis_index("sea") & 1
    span = by + 2 * SUB
    edge = wx * SUB
    lanes = depth.shape[1]
    near = near_edge[...].astype(jnp.float32)
    far = far_edge[...].astype(jnp.float32)
    prev = jnp.where(odd == 1, near, far)
    post = jnp.where(odd == 1, far, near)
    prev_d = joined(prev[edge:], lanes // 4)[by - SUB :]
    post_d = joined(post[edge:], lanes // 4)[0:SUB]
    d = jnp.concatenate([prev_d, depth[...], post_d], axis=0)
    east = jnp.minimum(d, pltpu.roll(d, lanes - 1, 1))
    north = jnp.minimum(d, pltpu.roll(d, span - 1, 0))
    wet = jnp.where(d > 0.0, 1.0, 0.0)
    zero = jnp.zeros((span, lanes), jnp.float32)
    for x in range(wx):
        column = jnp.concatenate(
            [prev[x * SUB : (x + 1) * SUB], total[x * by : (x + 1) * by], post[x * SUB : (x + 1) * SUB]],
            axis=0,
        )
        h[x] = column * jnp.broadcast_to(wet[:, x : x + 1], (span, lanes))
        de[x] = jnp.broadcast_to(east[:, x : x + 1], (span, lanes))
        dn[x] = jnp.broadcast_to(north[:, x : x + 1], (span, lanes))
        e[x] = zero
        n[x] = zero
    for step in range(STEPS):
        h_here = h[step]
        flux_before = None
        for x in range(step, wx - 1 - step):
            h_next = h[x + 1]
            new_east = e[x] - gravity_step * (h_next - h_here)
            e[x] = new_east
            flux = de[x] * new_east
            if flux_before is not None:
                new_north = n[x] - gravity_step * (pltpu.roll(h_here, span - 1, 0) - h_here)
                n[x] = new_north
                flux_north = dn[x] * new_north
                change = ((flux - flux_before) + flux_north) - pltpu.roll(flux_north, 1, 0)
                h[x] = h_here - height_step * change
            flux_before = flux
            h_here = h_next
    for y in range(by):
        level[y] = jnp.concatenate(
            [h[halo + x, SUB + y : SUB + y + 1, :] for x in range(bx)], axis=0
        )


def on_device(
    slip_rate,
    near_blocks,
    near_rows,
    near_cols,
    near_scale,
    far_left,
    far_right,
    far_rows,
    far_cols,
    far_rank,
    far_scale,
    sea_depth,
    wet_mask,
):
    by, bx = sea_depth.shape
    n_sea = lax.axis_size("sea")
    n_fault = lax.axis_size("fault")
    n_near = near_blocks.shape[2]
    n_far, rank, leaf = far_left.shape[2:]
    rows, members = slip_rate.shape
    leaf_count = by * bx * n_fault // leaf
    wx = bx + 2 * STEPS
    f32, bf16 = jnp.float32, jnp.bfloat16

    across = {}
    for k in range(2, n_sea, 2):
        across[k] = swap(slip_rate, "sea", k)
    across[1] = swap(slip_rate, "sea", 1)
    for k in range(2, n_sea, 2):
        across[k + 1] = swap(across[k], "sea", 1)

    vector = pl.BlockSpec(memory_space=pltpu.VMEM)
    scalar = pl.BlockSpec(memory_space=pltpu.SMEM)
    outside = pl.BlockSpec(memory_space=pltpu.HBM)
    short = [near_rows, near_cols, near_scale, far_rows, far_cols, far_rank, far_scale]
    short = [a[0] for a in short] + [sea_depth, wet_mask]
    heavy = [slip_rate, near_blocks[0, 0], far_left[0, 0], far_right[0, 0]]
    moved = sum(a.size * 2 for a in heavy)
    tables, scales, tile, mine, near, left, right = pl.pallas_call(
        fetch_kernel,
        out_shape=[
            jax.ShapeDtypeStruct((SUB, LANES), jnp.int32),
            jax.ShapeDtypeStruct((SUB, LANES), f32),
            jax.ShapeDtypeStruct((by, LANES), f32),
        ]
        + [jax.ShapeDtypeStruct(a.shape, bf16) for a in heavy],
        in_specs=[outside] * 13,
        out_specs=[vector] * 7,
        scratch_shapes=[pltpu.VMEM(a.shape, a.dtype) for a in short]
        + [pltpu.SemaphoreType.DMA((13,))],
        compiler_params=pltpu.CompilerParams(vmem_limit_bytes=4 << 20),
        cost_estimate=pl.CostEstimate(flops=0, bytes_accessed=2 * moved, transcendentals=0),
        name="fetch",
    )(*[pltpu.with_memory_space_constraint(a, pltpu.HBM) for a in short + heavy])
    slots = [mine] + [across[k] for k in range(1, n_sea)]
    cells = wx * by
    dims = (n_sea, n_fault, n_near, n_far, leaf, rank, rows, leaf_count, bx, wx)
    own, *chunks = pl.pallas_call(
        functools.partial(blocks_kernel, dims),
        out_shape=[jax.ShapeDtypeStruct((cells, members), f32)]
        + [jax.ShapeDtypeStruct((cells + by, members), bf16)] * (n_fault - 1),
        in_specs=[scalar] * 2 + [vector] * (n_sea + 4),
        out_specs=[vector] * n_fault,
        scratch_shapes=[
            pltpu.VMEM((n_sea * rows, members), bf16),
            pltpu.VMEM((n_far, rank, members), bf16),
            pltpu.VMEM((leaf_count * leaf, members), f32),
            pltpu.VMEM((n_fault * bx + 2 * STEPS, by, members), f32),
        ],
        compiler_params=pltpu.CompilerParams(vmem_limit_bytes=12 << 20),
        name="blocks",
    )(
        tables,
        scales,
        tile,
        *slots,
        near,
        left,
        right,
    )

    got = []
    for k in range(1, n_fault):
        got.append(swap(chunks[k - 1], "fault", k))

    edge = jax.ShapeDtypeStruct((wx * SUB + by, members), bf16)
    total, depth, uplift, near_edge, far_edge = pl.pallas_call(
        functools.partial(sum_kernel, (n_fault, bx, wx, by)),
        out_shape=[
            jax.ShapeDtypeStruct((cells, members), f32),
            jax.ShapeDtypeStruct((by, members), f32),
            jax.ShapeDtypeStruct((by, bx, members), f32),
            edge,
            edge,
        ],
        in_specs=[vector] * (1 + n_fault),
        out_specs=[vector] * 5,
        compiler_params=pltpu.CompilerParams(vmem_limit_bytes=8 << 20),
        name="sums",
    )(tile, own, *got)

    pairs = [(i, i + 1) for i in range(1, n_sea - 1, 2)]
    far_edge = lax.ppermute(far_edge, "sea", pairs + [(b, a) for a, b in pairs])
    near_edge = swap(near_edge, "sea", 1)

    span = by + 2 * SUB
    field = pltpu.VMEM((wx, span, members), f32)
    level = pl.pallas_call(
        functools.partial(steps_kernel, (bx, wx, by)),
        out_shape=jax.ShapeDtypeStruct((by, bx, members), f32),
        in_specs=[vector] * 4,
        out_specs=vector,
        scratch_shapes=[field] * 5,
        compiler_params=pltpu.CompilerParams(vmem_limit_bytes=8 << 20),
        name="steps",
    )(total, depth, near_edge, far_edge)
    return uplift, level


def solution(mesh):
    placed = (
        P(("fault", "sea"), None),
        P("sea", "fault", None, None, None),
        P("sea", "fault", None),
        P("sea", "fault", None),
        P("sea", "fault", None),
        P("sea", "fault", None, None, None),
        P("sea", "fault", None, None, None),
        P("sea", "fault", None),
        P("sea", "fault", None),
        P("sea", "fault", None),
        P("sea", "fault", None),
        P("sea", "fault"),
        P("sea", "fault"),
    )

    return jax.shard_map(
        on_device,
        mesh=mesh,
        in_specs=placed,
        out_specs=(P("sea", "fault", None), P("sea", "fault", None)),
        check_vma=False,
    )
```

```python
import functools

import jax
import jax.numpy as jnp
from jax import lax
from jax.experimental import pallas as pl
from jax.experimental.pallas import tpu as pltpu
from jax.sharding import PartitionSpec as P


STEPS = 6
SUB = 8
LANES = 128

gravity_step = 0.7
height_step = 0.7


def swap(x, axis, k):
    count = lax.axis_size(axis)
    return lax.ppermute(x, axis, [(i, i ^ k) for i in range(count)])


def pieces(d, gap):
    hi = d.astype(jnp.bfloat16).astype(jnp.float32)
    rest = d - hi
    mid = rest.astype(jnp.bfloat16).astype(jnp.float32)
    low = rest - mid
    packed = hi + pltpu.roll(mid, gap, 1) + pltpu.roll(low, 2 * gap, 1)
    return packed.astype(jnp.bfloat16)


def joined(tile, gap):
    t = tile.astype(jnp.float32)
    lanes = t.shape[1]
    d = (t + pltpu.roll(t, lanes - gap, 1)) + pltpu.roll(t, lanes - 2 * gap, 1)
    lane = lax.broadcasted_iota(jnp.int32, t.shape, 1)
    return jnp.where(lane < gap, d, 0.0)


def fetch_kernel(*refs):
    sources, refs = refs[:13], refs[13:]
    tables, scales, tile = refs[:3]
    targets, small, sems = refs[3:7], refs[7:16], refs[16]
    copies = [
        pltpu.make_async_copy(source, target, sems.at[k])
        for k, (source, target) in enumerate(zip(sources, small + targets))
    ]
    for copy in copies:
        copy.start()
    for copy in copies[:9]:
        copy.wait()
    near_rows, near_cols, near_scale, far_rows, far_cols, far_rank, far_scale = small[:7]
    for k, part in enumerate((near_rows, near_cols, far_rows, far_cols, far_rank)):
        tables[k : k + 1, 0 : part.shape[1]] = part[...]
    for k, part in enumerate((near_scale, far_scale)):
        scales[k : k + 1, 0 : part.shape[1]] = part[...]
    d = small[7][...] * small[8][...].astype(jnp.float32)
    by, bx = d.shape
    tile[...] = jnp.concatenate([d, jnp.zeros((by, LANES - bx), jnp.float32)], axis=1)
    for copy in copies[9:]:
        copy.wait()


def blocks_kernel(dims, *refs):
    n_sea, n_fault, n_near, n_far, leaf, rank, rows, leaf_count, bx, wx = dims
    tables, scales, tile = refs[:3]
    refs = refs[3:]
    slots = refs[:n_sea]
    near, left, right, own = refs[n_sea : 4 + n_sea]
    outs = refs[4 + n_sea : 3 + n_sea + n_fault]
    slip, coeffs, acc, wide = refs[3 + n_sea + n_fault :]
    sea = lax.axis_index("sea")
    fault = lax.axis_index("fault")
    members = slip.shape[1]
    by = tile.shape[0]
    width = leaf_count * leaf // by
    halo = (wx - bx) // 2
    for k in range(n_sea):
        start = pl.multiple_of((sea ^ k) * rows, rows)
        slip[pl.ds(start, rows)] = slots[k][...]
    acc[...] = jnp.zeros_like(acc)
    edge = jnp.zeros((halo,) + wide.shape[1:], jnp.float32)
    wide[0:halo] = edge
    wide[halo + width :] = edge
    level = lax.broadcasted_iota(jnp.int32, (rank, members), 0)
    for b in range(n_far):
        start = pl.multiple_of(tables[3, b] * leaf, leaf)
        c = jnp.dot(
            right[b], slip[pl.ds(start, leaf), :], preferred_element_type=jnp.float32
        )
        coeffs[b] = jnp.where(level < tables[4, b], c, 0.0).astype(jnp.bfloat16)
    for b in range(n_near):
        start = pl.multiple_of(tables[1, b] * leaf, leaf)
        target = pl.multiple_of(tables[0, b] * leaf, leaf)
        term = jnp.dot(
            near[b], slip[pl.ds(start, leaf), :], preferred_element_type=jnp.float32
        )
        acc[pl.ds(target, leaf), :] += scales[0, b] * term
    for b in range(n_far):
        target = pl.multiple_of(tables[2, b] * leaf, leaf)
        term = lax.dot_general(
            left[b], coeffs[b], (((0,), (0,)), ((), ())), preferred_element_type=jnp.float32
        )
        acc[pl.ds(target, leaf), :] += scales[1, b] * term
    wide[halo : halo + width] = jnp.swapaxes(acc[...].reshape(by, width, members), 0, 1)
    own[...] = wide[pl.ds(fault * bx, wx)].reshape(wx * by, members)
    packed = pieces(tile[...], bx)
    for k in range(1, n_fault):
        part = wide[pl.ds((fault ^ k) * bx, wx)].reshape(wx * by, members)
        outs[k - 1][0 : wx * by] = part.astype(jnp.bfloat16)
        outs[k - 1][wx * by :] = packed


def sum_kernel(dims, *refs):
    n_fault, bx, wx, by = dims
    tile, own = refs[:2]
    parts = refs[2 : 1 + n_fault]
    total, depth, near_edge, far_edge = refs[1 + n_fault :]
    sea = lax.axis_index("sea")
    fault = lax.axis_index("fault")
    halo = (wx - bx) // 2
    cells = wx * by
    s = own[...]
    for part in parts:
        s = s + part[0:cells].astype(jnp.float32)
    total[...] = s
    mid = tile[...]
    before = jnp.zeros_like(mid)
    after = jnp.zeros_like(mid)
    for k in range(1, n_fault):
        other = joined(parts[k - 1][cells:], bx)
        source = fault ^ k
        before = before + jnp.where(source == fault - 1, other, 0.0)
        after = after + jnp.where(source == fault + 1, other, 0.0)
    lanes = mid.shape[1]
    lane = lax.broadcasted_iota(jnp.int32, mid.shape, 1)
    d = jnp.where(lane < halo, pltpu.roll(before, lanes - (bx - halo), 1), 0.0)
    d = d + pltpu.roll(mid, halo, 1)
    d = d + pltpu.roll(jnp.where(lane < halo, after, 0.0), halo + bx, 1)
    depth[...] = d
    packed = pieces(d, lanes // 4)
    odd = sea & 1
    stack = s.reshape(wx, by, s.shape[1])
    first = stack[:, 0:SUB, :].reshape(wx * SUB, -1).astype(jnp.bfloat16)
    last = stack[:, by - SUB :, :].reshape(wx * SUB, -1).astype(jnp.bfloat16)
    near_edge[0 : wx * SUB] = jnp.where(odd == 1, first, last)
    far_edge[0 : wx * SUB] = jnp.where(odd == 1, last, first)
    near_edge[wx * SUB :] = packed
    far_edge[wx * SUB :] = packed


def uplift_kernel(dims, total, depth, uplift, wet):
    bx, wx, by = dims
    halo = (wx - bx) // 2
    across = jnp.transpose(jnp.where(depth[...] > 0.0, 1.0, 0.0))[halo : halo + bx]
    for y in range(by):
        wet[y] = jnp.broadcast_to(across[:, y : y + 1], wet.shape[1:])
    for y in range(by):
        uplift[y] = total[pl.ds(halo * by + y, bx, stride=by), :]


def steps_kernel(dims, total, depth, wet, near_edge, far_edge, level, column, rows):
    bx, wx, by = dims
    halo = (wx - bx) // 2
    odd = lax.axis_index("sea") & 1
    span = by + 2 * SUB
    folds = span // SUB
    edge = wx * SUB
    lanes = depth.shape[1]
    near = near_edge[...].astype(jnp.float32)
    far = far_edge[...].astype(jnp.float32)
    prev = jnp.where(odd == 1, near, far)
    post = jnp.where(odd == 1, far, near)
    prev_d = joined(prev[edge:], lanes // 4)[by - SUB :]
    post_d = joined(post[edge:], lanes // 4)[0:SUB]
    d = jnp.concatenate([prev_d, depth[...], post_d], axis=0)
    scale = gravity_step * height_step
    rows[0] = scale * jnp.minimum(d, pltpu.roll(d, lanes - 1, 1))
    rows[1] = scale * jnp.minimum(d, pltpu.roll(d, span - 1, 0))
    folded = [[rows[k, pl.ds(v, SUB, stride=folds), :] for v in range(folds)] for k in range(2)]

    def spread(part, x):
        return [jnp.broadcast_to(f[:, x : x + 1], (SUB, lanes)) for f in part]

    h = []
    for x in range(wx):
        base = x * span
        column[base : base + SUB] = prev[x * SUB : (x + 1) * SUB]
        column[base + SUB : base + SUB + by] = total[x * by : (x + 1) * by]
        column[base + SUB + by : base + span] = post[x * SUB : (x + 1) * SUB]
        h.append([column[pl.ds(base + v, SUB, stride=folds), :] for v in range(folds)])
    de = [spread(folded[0], x) for x in range(wx)]
    dn = [spread(folded[1], x) for x in range(wx)]
    e = [None] * wx
    n = [None] * wx
    for step in range(STEPS):
        before = None
        for x in range(step, wx - 1 - step):
            here = h[x]
            flow = [a - b for a, b in zip(here, h[x + 1])]
            if step:
                flow = [a + b for a, b in zip(e[x], flow)]
            e[x] = flow
            flux = [a * b for a, b in zip(de[x], flow)]
            if before is not None:
                up = here[1:] + [pltpu.roll(here[0], SUB - 1, 0)]
                flow = [a - b for a, b in zip(here, up)]
                if step:
                    flow = [a + b for a, b in zip(n[x], flow)]
                n[x] = flow
                rise = [a * b for a, b in zip(dn[x], flow)]
                down = [pltpu.roll(rise[-1], 1, 0)] + rise[:-1]
                h[x] = [
                    here[v] - (((flux[v] - before[v]) + rise[v]) - down[v])
                    for v in range(folds)
                ]
            before = flux
    for x in range(bx):
        for v in range(folds):
            column[pl.ds(x * span + v, SUB, stride=folds), :] = h[halo + x][v]
    for y in range(by):
        level[y] = wet[y] * column[pl.ds(SUB + y, bx, stride=span), :]


def on_device(
    slip_rate,
    near_blocks,
    near_rows,
    near_cols,
    near_scale,
    far_left,
    far_right,
    far_rows,
    far_cols,
    far_rank,
    far_scale,
    sea_depth,
    wet_mask,
):
    by, bx = sea_depth.shape
    n_sea = lax.axis_size("sea")
    n_fault = lax.axis_size("fault")
    n_near = near_blocks.shape[2]
    n_far, rank, leaf = far_left.shape[2:]
    rows, members = slip_rate.shape
    leaf_count = by * bx * n_fault // leaf
    wx = bx + 2 * STEPS
    f32, bf16 = jnp.float32, jnp.bfloat16

    across = {}
    for k in range(2, n_sea, 2):
        across[k] = swap(slip_rate, "sea", k)
    across[1] = swap(slip_rate, "sea", 1)
    for k in range(2, n_sea, 2):
        across[k + 1] = swap(across[k], "sea", 1)

    vector = pl.BlockSpec(memory_space=pltpu.VMEM)
    scalar = pl.BlockSpec(memory_space=pltpu.SMEM)
    outside = pl.BlockSpec(memory_space=pltpu.HBM)
    short = [near_rows, near_cols, near_scale, far_rows, far_cols, far_rank, far_scale]
    short = [a[0] for a in short] + [sea_depth, wet_mask]
    heavy = [slip_rate, near_blocks[0, 0], far_left[0, 0], far_right[0, 0]]
    moved = sum(a.size * 2 for a in heavy)
    tables, scales, tile, mine, near, left, right = pl.pallas_call(
        fetch_kernel,
        out_shape=[
            jax.ShapeDtypeStruct((SUB, LANES), jnp.int32),
            jax.ShapeDtypeStruct((SUB, LANES), f32),
            jax.ShapeDtypeStruct((by, LANES), f32),
        ]
        + [jax.ShapeDtypeStruct(a.shape, bf16) for a in heavy],
        in_specs=[outside] * 13,
        out_specs=[vector] * 7,
        scratch_shapes=[pltpu.VMEM(a.shape, a.dtype) for a in short]
        + [pltpu.SemaphoreType.DMA((13,))],
        compiler_params=pltpu.CompilerParams(vmem_limit_bytes=4 << 20),
        cost_estimate=pl.CostEstimate(flops=0, bytes_accessed=2 * moved, transcendentals=0),
        name="fetch",
    )(*[pltpu.with_memory_space_constraint(a, pltpu.HBM) for a in short + heavy])
    slots = [mine] + [across[k] for k in range(1, n_sea)]
    cells = wx * by
    dims = (n_sea, n_fault, n_near, n_far, leaf, rank, rows, leaf_count, bx, wx)
    own, *chunks = pl.pallas_call(
        functools.partial(blocks_kernel, dims),
        out_shape=[jax.ShapeDtypeStruct((cells, members), f32)]
        + [jax.ShapeDtypeStruct((cells + by, members), bf16)] * (n_fault - 1),
        in_specs=[scalar] * 2 + [vector] * (n_sea + 4),
        out_specs=[vector] * n_fault,
        scratch_shapes=[
            pltpu.VMEM((n_sea * rows, members), bf16),
            pltpu.VMEM((n_far, rank, members), bf16),
            pltpu.VMEM((leaf_count * leaf, members), f32),
            pltpu.VMEM((n_fault * bx + 2 * STEPS, by, members), f32),
        ],
        compiler_params=pltpu.CompilerParams(vmem_limit_bytes=12 << 20),
        name="blocks",
    )(
        tables,
        scales,
        tile,
        *slots,
        near,
        left,
        right,
    )

    got = []
    for k in range(1, n_fault):
        got.append(swap(chunks[k - 1], "fault", k))

    edge = jax.ShapeDtypeStruct((wx * SUB + by, members), bf16)
    total, depth, near_edge, far_edge = pl.pallas_call(
        functools.partial(sum_kernel, (n_fault, bx, wx, by)),
        out_shape=[
            jax.ShapeDtypeStruct((cells, members), f32),
            jax.ShapeDtypeStruct((by, members), f32),
            edge,
            edge,
        ],
        in_specs=[vector] * (1 + n_fault),
        out_specs=[vector] * 4,
        compiler_params=pltpu.CompilerParams(vmem_limit_bytes=8 << 20),
        name="sums",
    )(tile, own, *got)

    pairs = [(i, i + 1) for i in range(1, n_sea - 1, 2)]
    far_edge = lax.ppermute(far_edge, "sea", pairs + [(b, a) for a, b in pairs])
    near_edge = swap(near_edge, "sea", 1)

    uplift, wet = pl.pallas_call(
        functools.partial(uplift_kernel, (bx, wx, by)),
        out_shape=[jax.ShapeDtypeStruct((by, bx, members), f32)] * 2,
        in_specs=[vector] * 2,
        out_specs=[vector] * 2,
        compiler_params=pltpu.CompilerParams(vmem_limit_bytes=4 << 20),
        cost_estimate=pl.CostEstimate(flops=0, bytes_accessed=16 * cells * members, transcendentals=0),
        name="uplift",
    )(total, depth)
    span = by + 2 * SUB
    level = pl.pallas_call(
        functools.partial(steps_kernel, (bx, wx, by)),
        out_shape=jax.ShapeDtypeStruct((by, bx, members), f32),
        in_specs=[vector] * 5,
        out_specs=vector,
        scratch_shapes=[pltpu.VMEM((wx * span, members), f32), pltpu.VMEM((2, span, LANES), f32)],
        compiler_params=pltpu.CompilerParams(vmem_limit_bytes=8 << 20),
        name="steps",
    )(total, depth, wet, near_edge, far_edge)
    return uplift, level


def solution(mesh):
    placed = (
        P(("fault", "sea"), None),
        P("sea", "fault", None, None, None),
        P("sea", "fault", None),
        P("sea", "fault", None),
        P("sea", "fault", None),
        P("sea", "fault", None, None, None),
        P("sea", "fault", None, None, None),
        P("sea", "fault", None),
        P("sea", "fault", None),
        P("sea", "fault", None),
        P("sea", "fault", None),
        P("sea", "fault"),
        P("sea", "fault"),
    )

    return jax.shard_map(
        on_device,
        mesh=mesh,
        in_specs=placed,
        out_specs=(P("sea", "fault", None), P("sea", "fault", None)),
        check_vma=False,
    )
```

```python
import functools

import jax
import jax.numpy as jnp
from jax import lax
from jax.experimental import pallas as pl
from jax.experimental.pallas import tpu as pltpu
from jax.sharding import PartitionSpec as P


STEPS = 6
SUB = 8
LANES = 128

gravity_step = 0.7
height_step = 0.7


def swap(x, axis, k):
    count = lax.axis_size(axis)
    return lax.ppermute(x, axis, [(i, i ^ k) for i in range(count)])


def pieces(d, gap):
    hi = d.astype(jnp.bfloat16).astype(jnp.float32)
    rest = d - hi
    mid = rest.astype(jnp.bfloat16).astype(jnp.float32)
    low = rest - mid
    packed = hi + pltpu.roll(mid, gap, 1) + pltpu.roll(low, 2 * gap, 1)
    return packed.astype(jnp.bfloat16)


def joined(tile, gap):
    t = tile.astype(jnp.float32)
    lanes = t.shape[1]
    d = (t + pltpu.roll(t, lanes - gap, 1)) + pltpu.roll(t, lanes - 2 * gap, 1)
    lane = lax.broadcasted_iota(jnp.int32, t.shape, 1)
    return jnp.where(lane < gap, d, 0.0)


def tucked(tile):
    groups = tile.shape[0] // SUB
    t = tile.astype(jnp.float32)
    out = t[0:SUB]
    for g in range(1, groups):
        out = out + pltpu.roll(t[g * SUB : (g + 1) * SUB], g * LANES // groups, 1)
    return out.astype(jnp.bfloat16)


def untucked(tile, by, gap):
    groups = by // SUB
    t = tile.astype(jnp.float32)
    turned = [t] + [pltpu.roll(t, LANES - g * LANES // groups, 1) for g in range(1, groups)]
    return jnp.concatenate([joined(part, gap) for part in turned], axis=0)


def fetch_kernel(*refs):
    sources, refs = refs[:13], refs[13:]
    tables, scales, tile = refs[:3]
    targets, small, sems = refs[3:7], refs[7:16], refs[16]
    copies = [
        pltpu.make_async_copy(source, target, sems.at[k])
        for k, (source, target) in enumerate(zip(sources, small + targets))
    ]
    for copy in copies:
        copy.start()
    for copy in copies[:9]:
        copy.wait()
    near_rows, near_cols, near_scale, far_rows, far_cols, far_rank, far_scale = small[:7]
    for k, part in enumerate((near_rows, near_cols, far_rows, far_cols, far_rank)):
        tables[k : k + 1, 0 : part.shape[1]] = part[...]
    for k, part in enumerate((near_scale, far_scale)):
        scales[k : k + 1, 0 : part.shape[1]] = part[...]
    d = small[7][...] * small[8][...].astype(jnp.float32)
    by, bx = d.shape
    tile[...] = jnp.concatenate([d, jnp.zeros((by, LANES - bx), jnp.float32)], axis=1)
    for copy in copies[9:]:
        copy.wait()


def blocks_kernel(dims, *refs):
    n_sea, n_fault, n_near, n_far, leaf, rank, rows, leaf_count, bx, wx = dims
    tables, scales, tile = refs[:3]
    refs = refs[3:]
    slots = refs[:n_sea]
    near, left, right, own = refs[n_sea : 4 + n_sea]
    outs = refs[4 + n_sea : 3 + n_sea + n_fault]
    slip, coeffs, acc, wide = refs[3 + n_sea + n_fault :]
    sea = lax.axis_index("sea")
    fault = lax.axis_index("fault")
    members = slip.shape[1]
    by = tile.shape[0]
    width = leaf_count * leaf // by
    halo = (wx - bx) // 2
    for k in range(n_sea):
        start = pl.multiple_of((sea ^ k) * rows, rows)
        slip[pl.ds(start, rows)] = slots[k][...]
    acc[...] = jnp.zeros_like(acc)
    edge = jnp.zeros((halo,) + wide.shape[1:], jnp.float32)
    wide[0:halo] = edge
    wide[halo + width :] = edge
    level = lax.broadcasted_iota(jnp.int32, (rank, members), 0)
    for b in range(n_far):
        start = pl.multiple_of(tables[3, b] * leaf, leaf)
        c = jnp.dot(
            right[b], slip[pl.ds(start, leaf), :], preferred_element_type=jnp.float32
        )
        coeffs[b] = jnp.where(level < tables[4, b], c, 0.0).astype(jnp.bfloat16)
    for b in range(n_near):
        start = pl.multiple_of(tables[1, b] * leaf, leaf)
        target = pl.multiple_of(tables[0, b] * leaf, leaf)
        term = jnp.dot(
            near[b], slip[pl.ds(start, leaf), :], preferred_element_type=jnp.float32
        )
        acc[pl.ds(target, leaf), :] += scales[0, b] * term
    for b in range(n_far):
        target = pl.multiple_of(tables[2, b] * leaf, leaf)
        term = lax.dot_general(
            left[b], coeffs[b], (((0,), (0,)), ((), ())), preferred_element_type=jnp.float32
        )
        acc[pl.ds(target, leaf), :] += scales[1, b] * term
    wide[halo : halo + width] = jnp.swapaxes(acc[...].reshape(by, width, members), 0, 1)
    own[...] = wide[pl.ds(fault * bx, wx)].reshape(wx * by, members)
    packed = tucked(pieces(tile[...], bx))
    for k in range(1, n_fault):
        part = wide[pl.ds((fault ^ k) * bx, wx)].reshape(wx * by, members)
        outs[k - 1][0 : wx * by] = part.astype(jnp.bfloat16)
        outs[k - 1][wx * by :] = packed


def sum_kernel(dims, *refs):
    n_fault, bx, wx, by = dims
    tile, own = refs[:2]
    parts = refs[2 : 1 + n_fault]
    total, depth, near_edge, far_edge = refs[1 + n_fault :]
    sea = lax.axis_index("sea")
    fault = lax.axis_index("fault")
    halo = (wx - bx) // 2
    cells = wx * by
    s = own[...]
    for part in parts:
        s = s + part[0:cells].astype(jnp.float32)
    total[...] = s
    mid = tile[...]
    before = jnp.zeros_like(mid)
    after = jnp.zeros_like(mid)
    for k in range(1, n_fault):
        other = untucked(parts[k - 1][cells:], by, bx)
        source = fault ^ k
        before = before + jnp.where(source == fault - 1, other, 0.0)
        after = after + jnp.where(source == fault + 1, other, 0.0)
    lanes = mid.shape[1]
    lane = lax.broadcasted_iota(jnp.int32, mid.shape, 1)
    d = jnp.where(lane < halo, pltpu.roll(before, lanes - (bx - halo), 1), 0.0)
    d = d + pltpu.roll(mid, halo, 1)
    d = d + pltpu.roll(jnp.where(lane < halo, after, 0.0), halo + bx, 1)
    depth[...] = d
    packed = pieces(d, lanes // 4)
    odd = sea & 1
    stack = s.reshape(wx, by, s.shape[1])
    first = stack[:, 0:SUB, :].reshape(wx * SUB, -1).astype(jnp.bfloat16)
    last = stack[:, by - SUB :, :].reshape(wx * SUB, -1).astype(jnp.bfloat16)
    near_edge[0 : wx * SUB] = jnp.where(odd == 1, first, last)
    far_edge[0 : wx * SUB] = jnp.where(odd == 1, last, first)
    near_edge[wx * SUB :] = packed
    far_edge[wx * SUB :] = packed


def uplift_kernel(dims, total, depth, uplift, wet):
    bx, wx, by = dims
    halo = (wx - bx) // 2
    across = jnp.transpose(jnp.where(depth[...] > 0.0, 1.0, 0.0))[halo : halo + bx]
    for y in range(by):
        wet[y] = jnp.broadcast_to(across[:, y : y + 1], wet.shape[1:])
    for y in range(by):
        uplift[y] = total[pl.ds(halo * by + y, bx, stride=by), :]


def steps_kernel(dims, total, depth, wet, near_edge, far_edge, level, column, rows):
    bx, wx, by = dims
    halo = (wx - bx) // 2
    sea = lax.axis_index("sea")
    odd = sea & 1
    span = by + 2 * SUB
    folds = span // SUB
    edge = wx * SUB
    lanes = depth.shape[1]
    near = near_edge[...].astype(jnp.float32)
    far = far_edge[...].astype(jnp.float32)
    prev = jnp.where(odd == 1, near, far)
    post = jnp.where(odd == 1, far, near)
    prev_d = joined(prev[edge:], lanes // 4)[by - SUB :]
    post_d = joined(post[edge:], lanes // 4)[0:SUB]
    prev_d = jnp.where(sea == 0, 0.0, prev_d)
    post_d = jnp.where(sea == lax.axis_size("sea") - 1, 0.0, post_d)
    d = jnp.concatenate([prev_d, depth[...], post_d], axis=0)
    scale = gravity_step * height_step
    rows[0] = scale * jnp.minimum(d, pltpu.roll(d, lanes - 1, 1))
    rows[1] = scale * jnp.minimum(d, pltpu.roll(d, span - 1, 0))
    folded = [[rows[k, pl.ds(v, SUB, stride=folds), :] for v in range(folds)] for k in range(2)]

    def spread(part, x):
        return [jnp.broadcast_to(f[:, x : x + 1], (SUB, lanes)) for f in part]

    h = []
    for x in range(wx):
        base = x * span
        column[base : base + SUB] = prev[x * SUB : (x + 1) * SUB]
        column[base + SUB : base + SUB + by] = total[x * by : (x + 1) * by]
        column[base + SUB + by : base + span] = post[x * SUB : (x + 1) * SUB]
        h.append([column[pl.ds(base + v, SUB, stride=folds), :] for v in range(folds)])
    de = [spread(folded[0], x) for x in range(wx)]
    dn = [spread(folded[1], x) for x in range(wx)]
    e = [None] * wx
    n = [None] * wx
    for step in range(STEPS):
        before = None
        for x in range(step, wx - 1 - step):
            here = h[x]
            flow = [a - b for a, b in zip(here, h[x + 1])]
            if step:
                flow = [a + b for a, b in zip(e[x], flow)]
            e[x] = flow
            flux = [a * b for a, b in zip(de[x], flow)]
            if before is not None:
                up = here[1:] + [pltpu.roll(here[0], SUB - 1, 0)]
                flow = [a - b for a, b in zip(here, up)]
                if step:
                    flow = [a + b for a, b in zip(n[x], flow)]
                n[x] = flow
                rise = [a * b for a, b in zip(dn[x], flow)]
                down = [pltpu.roll(rise[-1], 1, 0)] + rise[:-1]
                h[x] = [
                    here[v] - (((flux[v] - before[v]) + rise[v]) - down[v])
                    for v in range(folds)
                ]
            before = flux
    for x in range(bx):
        for v in range(folds):
            column[pl.ds(x * span + v, SUB, stride=folds), :] = h[halo + x][v]
    for y in range(by):
        level[y] = wet[y] * column[pl.ds(SUB + y, bx, stride=span), :]


def on_device(
    slip_rate,
    near_blocks,
    near_rows,
    near_cols,
    near_scale,
    far_left,
    far_right,
    far_rows,
    far_cols,
    far_rank,
    far_scale,
    sea_depth,
    wet_mask,
):
    by, bx = sea_depth.shape
    n_sea = lax.axis_size("sea")
    n_fault = lax.axis_size("fault")
    n_near = near_blocks.shape[2]
    n_far, rank, leaf = far_left.shape[2:]
    rows, members = slip_rate.shape
    leaf_count = by * bx * n_fault // leaf
    wx = bx + 2 * STEPS
    f32, bf16 = jnp.float32, jnp.bfloat16

    across = {}
    for k in range(2, n_sea, 2):
        across[k] = swap(slip_rate, "sea", k)
    across[1] = swap(slip_rate, "sea", 1)
    for k in range(2, n_sea, 2):
        across[k + 1] = swap(across[k], "sea", 1)

    vector = pl.BlockSpec(memory_space=pltpu.VMEM)
    scalar = pl.BlockSpec(memory_space=pltpu.SMEM)
    outside = pl.BlockSpec(memory_space=pltpu.HBM)
    short = [near_rows, near_cols, near_scale, far_rows, far_cols, far_rank, far_scale]
    short = [a[0] for a in short] + [sea_depth, wet_mask]
    heavy = [slip_rate, near_blocks[0, 0], far_left[0, 0], far_right[0, 0]]
    moved = sum(a.size * 2 for a in heavy)
    tables, scales, tile, mine, near, left, right = pl.pallas_call(
        fetch_kernel,
        out_shape=[
            jax.ShapeDtypeStruct((SUB, LANES), jnp.int32),
            jax.ShapeDtypeStruct((SUB, LANES), f32),
            jax.ShapeDtypeStruct((by, LANES), f32),
        ]
        + [jax.ShapeDtypeStruct(a.shape, bf16) for a in heavy],
        in_specs=[outside] * 13,
        out_specs=[vector] * 7,
        scratch_shapes=[pltpu.VMEM(a.shape, a.dtype) for a in short]
        + [pltpu.SemaphoreType.DMA((13,))],
        compiler_params=pltpu.CompilerParams(vmem_limit_bytes=4 << 20),
        cost_estimate=pl.CostEstimate(flops=0, bytes_accessed=2 * moved, transcendentals=0),
        name="fetch",
    )(*[pltpu.with_memory_space_constraint(a, pltpu.HBM) for a in short + heavy])
    slots = [mine] + [across[k] for k in range(1, n_sea)]
    cells = wx * by
    dims = (n_sea, n_fault, n_near, n_far, leaf, rank, rows, leaf_count, bx, wx)
    own, *chunks = pl.pallas_call(
        functools.partial(blocks_kernel, dims),
        out_shape=[jax.ShapeDtypeStruct((cells, members), f32)]
        + [jax.ShapeDtypeStruct((cells + SUB, members), bf16)] * (n_fault - 1),
        in_specs=[scalar] * 2 + [vector] * (n_sea + 4),
        out_specs=[vector] * n_fault,
        scratch_shapes=[
            pltpu.VMEM((n_sea * rows, members), bf16),
            pltpu.VMEM((n_far, rank, members), bf16),
            pltpu.VMEM((leaf_count * leaf, members), f32),
            pltpu.VMEM((n_fault * bx + 2 * STEPS, by, members), f32),
        ],
        compiler_params=pltpu.CompilerParams(vmem_limit_bytes=12 << 20),
        name="blocks",
    )(
        tables,
        scales,
        tile,
        *slots,
        near,
        left,
        right,
    )

    got = []
    for k in range(1, n_fault):
        got.append(swap(chunks[k - 1], "fault", k))

    edge = jax.ShapeDtypeStruct((wx * SUB + by, members), bf16)
    total, depth, near_edge, far_edge = pl.pallas_call(
        functools.partial(sum_kernel, (n_fault, bx, wx, by)),
        out_shape=[
            jax.ShapeDtypeStruct((cells, members), f32),
            jax.ShapeDtypeStruct((by, members), f32),
            edge,
            edge,
        ],
        in_specs=[vector] * (1 + n_fault),
        out_specs=[vector] * 4,
        compiler_params=pltpu.CompilerParams(vmem_limit_bytes=8 << 20),
        name="sums",
    )(tile, own, *got)

    ring = []
    for i in range(n_sea):
        j = i + 2 * (i & 1) - 1
        for f in range(n_fault):
            inside = 0 <= j < n_sea
            ring.append((i * n_fault + f, j * n_fault + f if inside else i * n_fault + (f ^ 1)))
    far_edge = lax.ppermute(far_edge, ("sea", "fault"), ring)
    near_edge = swap(near_edge, "sea", 1)

    uplift, wet = pl.pallas_call(
        functools.partial(uplift_kernel, (bx, wx, by)),
        out_shape=[jax.ShapeDtypeStruct((by, bx, members), f32)] * 2,
        in_specs=[vector] * 2,
        out_specs=[vector] * 2,
        compiler_params=pltpu.CompilerParams(vmem_limit_bytes=4 << 20),
        cost_estimate=pl.CostEstimate(flops=0, bytes_accessed=16 * cells * members, transcendentals=0),
        name="uplift",
    )(total, depth)
    span = by + 2 * SUB
    level = pl.pallas_call(
        functools.partial(steps_kernel, (bx, wx, by)),
        out_shape=jax.ShapeDtypeStruct((by, bx, members), f32),
        in_specs=[vector] * 5,
        out_specs=vector,
        scratch_shapes=[pltpu.VMEM((wx * span, members), f32), pltpu.VMEM((2, span, LANES), f32)],
        compiler_params=pltpu.CompilerParams(vmem_limit_bytes=8 << 20),
        name="steps",
    )(total, depth, wet, near_edge, far_edge)
    return uplift, level


def solution(mesh):
    placed = (
        P(("fault", "sea"), None),
        P("sea", "fault", None, None, None),
        P("sea", "fault", None),
        P("sea", "fault", None),
        P("sea", "fault", None),
        P("sea", "fault", None, None, None),
        P("sea", "fault", None, None, None),
        P("sea", "fault", None),
        P("sea", "fault", None),
        P("sea", "fault", None),
        P("sea", "fault", None),
        P("sea", "fault"),
        P("sea", "fault"),
    )

    return jax.shard_map(
        on_device,
        mesh=mesh,
        in_specs=placed,
        out_specs=(P("sea", "fault", None), P("sea", "fault", None)),
        check_vma=False,
    )
```

```python
import functools

import jax
import jax.numpy as jnp
from jax import lax
from jax.experimental import pallas as pl
from jax.experimental.pallas import tpu as pltpu
from jax.sharding import PartitionSpec as P


STEPS = 6
SUB = 8
LANES = 128

gravity_step = 0.7
height_step = 0.7


def swap(x, axis, k):
    count = lax.axis_size(axis)
    return lax.ppermute(x, axis, [(i, i ^ k) for i in range(count)])


def pieces(d, gap):
    hi = d.astype(jnp.bfloat16).astype(jnp.float32)
    rest = d - hi
    mid = rest.astype(jnp.bfloat16).astype(jnp.float32)
    low = rest - mid
    packed = hi + pltpu.roll(mid, gap, 1) + pltpu.roll(low, 2 * gap, 1)
    return packed.astype(jnp.bfloat16)


def joined(tile, gap):
    t = tile.astype(jnp.float32)
    lanes = t.shape[1]
    d = (t + pltpu.roll(t, lanes - gap, 1)) + pltpu.roll(t, lanes - 2 * gap, 1)
    lane = lax.broadcasted_iota(jnp.int32, t.shape, 1)
    return jnp.where(lane < gap, d, 0.0)


def tucked(tile):
    groups = tile.shape[0] // SUB
    t = tile.astype(jnp.float32)
    out = t[0:SUB]
    for g in range(1, groups):
        out = out + pltpu.roll(t[g * SUB : (g + 1) * SUB], g * LANES // groups, 1)
    return out.astype(jnp.bfloat16)


def untucked(tile, by, gap):
    groups = by // SUB
    t = tile.astype(jnp.float32)
    turned = [t] + [pltpu.roll(t, LANES - g * LANES // groups, 1) for g in range(1, groups)]
    return jnp.concatenate([joined(part, gap) for part in turned], axis=0)


def fetch_kernel(*refs):
    sources, refs = refs[:13], refs[13:]
    tables, scales, tile = refs[:3]
    targets, small, sems = refs[3:7], refs[7:16], refs[16]
    copies = [
        pltpu.make_async_copy(source, target, sems.at[k])
        for k, (source, target) in enumerate(zip(sources, small + targets))
    ]
    for copy in copies:
        copy.start()
    for copy in copies[:9]:
        copy.wait()
    near_rows, near_cols, near_scale, far_rows, far_cols, far_rank, far_scale = small[:7]
    for k, part in enumerate((near_rows, near_cols, far_rows, far_cols, far_rank)):
        tables[k : k + 1, 0 : part.shape[1]] = part[...]
    for k, part in enumerate((near_scale, far_scale)):
        scales[k : k + 1, 0 : part.shape[1]] = part[...]
    d = small[7][...] * small[8][...].astype(jnp.float32)
    by, bx = d.shape
    tile[...] = jnp.concatenate([d, jnp.zeros((by, LANES - bx), jnp.float32)], axis=1)
    for copy in copies[9:]:
        copy.wait()


def blocks_kernel(dims, *refs):
    n_sea, n_fault, n_near, n_far, leaf, rank, rows, leaf_count, bx, wx = dims
    tables, scales, tile = refs[:3]
    refs = refs[3:]
    slots = refs[:n_sea]
    near, left, right, own = refs[n_sea : 4 + n_sea]
    outs = refs[4 + n_sea : 3 + n_sea + n_fault]
    rims = refs[3 + n_sea + n_fault : 2 + n_sea + 2 * n_fault]
    slip, coeffs, acc, wide = refs[2 + n_sea + 2 * n_fault :]
    sea = lax.axis_index("sea")
    fault = lax.axis_index("fault")
    members = slip.shape[1]
    by = tile.shape[0]
    width = leaf_count * leaf // by
    halo = (wx - bx) // 2
    for k in range(n_sea):
        start = pl.multiple_of((sea ^ k) * rows, rows)
        slip[pl.ds(start, rows)] = slots[k][...]
    acc[...] = jnp.zeros_like(acc)
    edge = jnp.zeros((halo,) + wide.shape[1:], jnp.float32)
    wide[0:halo] = edge
    wide[halo + width :] = edge
    level = lax.broadcasted_iota(jnp.int32, (rank, members), 0)
    for b in range(n_far):
        start = pl.multiple_of(tables[3, b] * leaf, leaf)
        c = jnp.dot(
            right[b], slip[pl.ds(start, leaf), :], preferred_element_type=jnp.float32
        )
        coeffs[b] = jnp.where(level < tables[4, b], c, 0.0).astype(jnp.bfloat16)
    for b in range(n_near):
        start = pl.multiple_of(tables[1, b] * leaf, leaf)
        target = pl.multiple_of(tables[0, b] * leaf, leaf)
        term = jnp.dot(
            near[b], slip[pl.ds(start, leaf), :], preferred_element_type=jnp.float32
        )
        acc[pl.ds(target, leaf), :] += scales[0, b] * term
    for b in range(n_far):
        target = pl.multiple_of(tables[2, b] * leaf, leaf)
        term = lax.dot_general(
            left[b], coeffs[b], (((0,), (0,)), ((), ())), preferred_element_type=jnp.float32
        )
        acc[pl.ds(target, leaf), :] += scales[1, b] * term
    wide[halo : halo + width] = jnp.swapaxes(acc[...].reshape(by, width, members), 0, 1)
    own[...] = wide[pl.ds(fault * bx, wx)].reshape(wx * by, members)
    packed = tucked(pieces(tile[...], bx))
    reach = bx + halo
    for k in range(1, n_fault):
        target = fault ^ k
        start = target * bx
        base = start + jnp.where(target == 0, halo, 0)
        part = wide[pl.ds(base, reach)].reshape(reach * by, members)
        outs[k - 1][0 : reach * by] = part.astype(jnp.bfloat16)
        outs[k - 1][reach * by :] = packed
        part = wide[pl.ds(start + reach, halo)].reshape(halo * by, members)
        rims[k - 1][...] = part.astype(jnp.bfloat16)


def sum_kernel(dims, *refs):
    n_fault, bx, wx, by = dims
    tile, own = refs[:2]
    parts = refs[2 : 1 + n_fault]
    rims = refs[1 + n_fault : 2 * n_fault]
    total, depth, near_edge, far_edge = refs[2 * n_fault :]
    sea = lax.axis_index("sea")
    fault = lax.axis_index("fault")
    halo = (wx - bx) // 2
    reach = (bx + halo) * by
    main = parts[0][0:reach].astype(jnp.float32)
    for part in parts[1:]:
        main = main + part[0:reach].astype(jnp.float32)
    side = rims[0][...].astype(jnp.float32)
    for rim in rims[1:]:
        side = side + rim[...].astype(jnp.float32)
    zero = jnp.zeros_like(side)
    side = jnp.where(fault == n_fault - 1, zero, side)
    inner = jnp.concatenate([main, side], axis=0)
    first = jnp.concatenate([zero, main], axis=0)
    s = own[...] + jnp.where(fault == 0, first, inner)
    total[...] = s
    mid = tile[...]
    before = jnp.zeros_like(mid)
    after = jnp.zeros_like(mid)
    for k in range(1, n_fault):
        other = untucked(parts[k - 1][reach:], by, bx)
        source = fault ^ k
        before = before + jnp.where(source == fault - 1, other, 0.0)
        after = after + jnp.where(source == fault + 1, other, 0.0)
    lanes = mid.shape[1]
    lane = lax.broadcasted_iota(jnp.int32, mid.shape, 1)
    d = jnp.where(lane < halo, pltpu.roll(before, lanes - (bx - halo), 1), 0.0)
    d = d + pltpu.roll(mid, halo, 1)
    d = d + pltpu.roll(jnp.where(lane < halo, after, 0.0), halo + bx, 1)
    depth[...] = d
    packed = pieces(d, lanes // 4)
    odd = sea & 1
    stack = s.reshape(wx, by, s.shape[1])
    first = stack[:, 0:SUB, :].reshape(wx * SUB, -1).astype(jnp.bfloat16)
    last = stack[:, by - SUB :, :].reshape(wx * SUB, -1).astype(jnp.bfloat16)
    near_edge[0 : wx * SUB] = jnp.where(odd == 1, first, last)
    far_edge[0 : wx * SUB] = jnp.where(odd == 1, last, first)
    near_edge[wx * SUB :] = packed
    far_edge[wx * SUB :] = packed


def uplift_kernel(dims, total, depth, uplift, wet):
    bx, wx, by = dims
    halo = (wx - bx) // 2
    across = jnp.transpose(jnp.where(depth[...] > 0.0, 1.0, 0.0))[halo : halo + bx]
    for y in range(by):
        wet[y] = jnp.broadcast_to(across[:, y : y + 1], wet.shape[1:])
    for y in range(by):
        uplift[y] = total[pl.ds(halo * by + y, bx, stride=by), :]


def steps_kernel(dims, total, depth, wet, near_edge, far_edge, level, column, rows):
    bx, wx, by = dims
    halo = (wx - bx) // 2
    sea = lax.axis_index("sea")
    odd = sea & 1
    span = by + 2 * SUB
    folds = span // SUB
    edge = wx * SUB
    lanes = depth.shape[1]
    near = near_edge[...].astype(jnp.float32)
    far = far_edge[...].astype(jnp.float32)
    prev = jnp.where(odd == 1, near, far)
    post = jnp.where(odd == 1, far, near)
    prev_d = joined(prev[edge:], lanes // 4)[by - SUB :]
    post_d = joined(post[edge:], lanes // 4)[0:SUB]
    prev_d = jnp.where(sea == 0, 0.0, prev_d)
    post_d = jnp.where(sea == lax.axis_size("sea") - 1, 0.0, post_d)
    d = jnp.concatenate([prev_d, depth[...], post_d], axis=0)
    scale = gravity_step * height_step
    rows[0] = scale * jnp.minimum(d, pltpu.roll(d, lanes - 1, 1))
    rows[1] = scale * jnp.minimum(d, pltpu.roll(d, span - 1, 0))
    folded = [[rows[k, pl.ds(v, SUB, stride=folds), :] for v in range(folds)] for k in range(2)]

    def spread(part, x):
        return [jnp.broadcast_to(f[:, x : x + 1], (SUB, lanes)) for f in part]

    h = []
    for x in range(wx):
        base = x * span
        column[base : base + SUB] = prev[x * SUB : (x + 1) * SUB]
        column[base + SUB : base + SUB + by] = total[x * by : (x + 1) * by]
        column[base + SUB + by : base + span] = post[x * SUB : (x + 1) * SUB]
        h.append([column[pl.ds(base + v, SUB, stride=folds), :] for v in range(folds)])
    de = [spread(folded[0], x) for x in range(wx)]
    dn = [spread(folded[1], x) for x in range(wx)]
    e = [None] * wx
    n = [None] * wx
    for step in range(STEPS):
        before = None
        for x in range(step, wx - 1 - step):
            here = h[x]
            flow = [a - b for a, b in zip(here, h[x + 1])]
            if step:
                flow = [a + b for a, b in zip(e[x], flow)]
            e[x] = flow
            flux = [a * b for a, b in zip(de[x], flow)]
            if before is not None:
                up = here[1:] + [pltpu.roll(here[0], SUB - 1, 0)]
                flow = [a - b for a, b in zip(here, up)]
                if step:
                    flow = [a + b for a, b in zip(n[x], flow)]
                n[x] = flow
                rise = [a * b for a, b in zip(dn[x], flow)]
                down = [pltpu.roll(rise[-1], 1, 0)] + rise[:-1]
                h[x] = [
                    here[v] - (((flux[v] - before[v]) + rise[v]) - down[v])
                    for v in range(folds)
                ]
            before = flux
    for x in range(bx):
        for v in range(folds):
            column[pl.ds(x * span + v, SUB, stride=folds), :] = h[halo + x][v]
    for y in range(by):
        level[y] = wet[y] * column[pl.ds(SUB + y, bx, stride=span), :]


def on_device(
    slip_rate,
    near_blocks,
    near_rows,
    near_cols,
    near_scale,
    far_left,
    far_right,
    far_rows,
    far_cols,
    far_rank,
    far_scale,
    sea_depth,
    wet_mask,
):
    by, bx = sea_depth.shape
    n_sea = lax.axis_size("sea")
    n_fault = lax.axis_size("fault")
    n_near = near_blocks.shape[2]
    n_far, rank, leaf = far_left.shape[2:]
    rows, members = slip_rate.shape
    leaf_count = by * bx * n_fault // leaf
    wx = bx + 2 * STEPS
    f32, bf16 = jnp.float32, jnp.bfloat16

    across = {}
    for k in range(2, n_sea, 2):
        across[k] = swap(slip_rate, "sea", k)
    across[1] = swap(slip_rate, "sea", 1)
    for k in range(2, n_sea, 2):
        across[k + 1] = swap(across[k], "sea", 1)

    vector = pl.BlockSpec(memory_space=pltpu.VMEM)
    scalar = pl.BlockSpec(memory_space=pltpu.SMEM)
    outside = pl.BlockSpec(memory_space=pltpu.HBM)
    short = [near_rows, near_cols, near_scale, far_rows, far_cols, far_rank, far_scale]
    short = [a[0] for a in short] + [sea_depth, wet_mask]
    heavy = [slip_rate, near_blocks[0, 0], far_left[0, 0], far_right[0, 0]]
    moved = sum(a.size * 2 for a in heavy)
    tables, scales, tile, mine, near, left, right = pl.pallas_call(
        fetch_kernel,
        out_shape=[
            jax.ShapeDtypeStruct((SUB, LANES), jnp.int32),
            jax.ShapeDtypeStruct((SUB, LANES), f32),
            jax.ShapeDtypeStruct((by, LANES), f32),
        ]
        + [jax.ShapeDtypeStruct(a.shape, bf16) for a in heavy],
        in_specs=[outside] * 13,
        out_specs=[vector] * 7,
        scratch_shapes=[pltpu.VMEM(a.shape, a.dtype) for a in short]
        + [pltpu.SemaphoreType.DMA((13,))],
        compiler_params=pltpu.CompilerParams(vmem_limit_bytes=4 << 20),
        cost_estimate=pl.CostEstimate(flops=0, bytes_accessed=2 * moved, transcendentals=0),
        name="fetch",
    )(*[pltpu.with_memory_space_constraint(a, pltpu.HBM) for a in short + heavy])
    slots = [mine] + [across[k] for k in range(1, n_sea)]
    cells = wx * by
    dims = (n_sea, n_fault, n_near, n_far, leaf, rank, rows, leaf_count, bx, wx)
    own, *chunks = pl.pallas_call(
        functools.partial(blocks_kernel, dims),
        out_shape=[jax.ShapeDtypeStruct((cells, members), f32)]
        + [jax.ShapeDtypeStruct(((bx + STEPS) * by + SUB, members), bf16)] * (n_fault - 1)
        + [jax.ShapeDtypeStruct((STEPS * by, members), bf16)] * (n_fault - 1),
        in_specs=[scalar] * 2 + [vector] * (n_sea + 4),
        out_specs=[vector] * (2 * n_fault - 1),
        scratch_shapes=[
            pltpu.VMEM((n_sea * rows, members), bf16),
            pltpu.VMEM((n_far, rank, members), bf16),
            pltpu.VMEM((leaf_count * leaf, members), f32),
            pltpu.VMEM((n_fault * bx + 2 * STEPS, by, members), f32),
        ],
        compiler_params=pltpu.CompilerParams(vmem_limit_bytes=12 << 20),
        name="blocks",
    )(
        tables,
        scales,
        tile,
        *slots,
        near,
        left,
        right,
    )

    got = []
    for k in range(1, n_fault):
        got.append(swap(chunks[k - 1], "fault", k))
    last = n_fault - 1
    for k in range(1, n_fault):
        hops = []
        for i in range(n_sea):
            for f in range(n_fault):
                j, g = i, f ^ k
                if g in (0, last) and k == last:
                    j, g = i ^ 1, f
                elif g in (0, last) and last < 2 * k:
                    g = last - g
                hops.append((i * n_fault + f, j * n_fault + g))
        got.append(lax.ppermute(chunks[last + k - 1], ("sea", "fault"), hops))

    edge = jax.ShapeDtypeStruct((wx * SUB + by, members), bf16)
    total, depth, near_edge, far_edge = pl.pallas_call(
        functools.partial(sum_kernel, (n_fault, bx, wx, by)),
        out_shape=[
            jax.ShapeDtypeStruct((cells, members), f32),
            jax.ShapeDtypeStruct((by, members), f32),
            edge,
            edge,
        ],
        in_specs=[vector] * (2 * n_fault),
        out_specs=[vector] * 4,
        compiler_params=pltpu.CompilerParams(vmem_limit_bytes=8 << 20),
        name="sums",
    )(tile, own, *got)

    ring = []
    for i in range(n_sea):
        j = i + 2 * (i & 1) - 1
        for f in range(n_fault):
            inside = 0 <= j < n_sea
            ring.append((i * n_fault + f, j * n_fault + f if inside else i * n_fault + (f ^ 1)))
    far_edge = lax.ppermute(far_edge, ("sea", "fault"), ring)
    near_edge = swap(near_edge, "sea", 1)

    uplift, wet = pl.pallas_call(
        functools.partial(uplift_kernel, (bx, wx, by)),
        out_shape=[jax.ShapeDtypeStruct((by, bx, members), f32)] * 2,
        in_specs=[vector] * 2,
        out_specs=[vector] * 2,
        compiler_params=pltpu.CompilerParams(vmem_limit_bytes=4 << 20),
        cost_estimate=pl.CostEstimate(flops=0, bytes_accessed=16 * cells * members, transcendentals=0),
        name="uplift",
    )(total, depth)
    span = by + 2 * SUB
    level = pl.pallas_call(
        functools.partial(steps_kernel, (bx, wx, by)),
        out_shape=jax.ShapeDtypeStruct((by, bx, members), f32),
        in_specs=[vector] * 5,
        out_specs=vector,
        scratch_shapes=[pltpu.VMEM((wx * span, members), f32), pltpu.VMEM((2, span, LANES), f32)],
        compiler_params=pltpu.CompilerParams(vmem_limit_bytes=8 << 20),
        name="steps",
    )(total, depth, wet, near_edge, far_edge)
    return uplift, level


def solution(mesh):
    placed = (
        P(("fault", "sea"), None),
        P("sea", "fault", None, None, None),
        P("sea", "fault", None),
        P("sea", "fault", None),
        P("sea", "fault", None),
        P("sea", "fault", None, None, None),
        P("sea", "fault", None, None, None),
        P("sea", "fault", None),
        P("sea", "fault", None),
        P("sea", "fault", None),
        P("sea", "fault", None),
        P("sea", "fault"),
        P("sea", "fault"),
    )

    return jax.shard_map(
        on_device,
        mesh=mesh,
        in_specs=placed,
        out_specs=(P("sea", "fault", None), P("sea", "fault", None)),
        check_vma=False,
    )
```

```python
import functools

import jax
import jax.numpy as jnp
from jax import lax
from jax.experimental import pallas as pl
from jax.experimental.pallas import tpu as pltpu
from jax.sharding import PartitionSpec as P


STEPS = 6
SUB = 8
LANES = 128

gravity_step = 0.7
height_step = 0.7


def swap(x, axis, k):
    count = lax.axis_size(axis)
    return lax.ppermute(x, axis, [(i, i ^ k) for i in range(count)])


def pieces(d, gap):
    hi = d.astype(jnp.bfloat16).astype(jnp.float32)
    rest = d - hi
    mid = rest.astype(jnp.bfloat16).astype(jnp.float32)
    low = rest - mid
    packed = hi + pltpu.roll(mid, gap, 1) + pltpu.roll(low, 2 * gap, 1)
    return packed.astype(jnp.bfloat16)


def joined(tile, gap):
    t = tile.astype(jnp.float32)
    lanes = t.shape[1]
    d = (t + pltpu.roll(t, lanes - gap, 1)) + pltpu.roll(t, lanes - 2 * gap, 1)
    lane = lax.broadcasted_iota(jnp.int32, t.shape, 1)
    return jnp.where(lane < gap, d, 0.0)


def beside(k):
    return k & (k + 1) == 0


def tucked(tile):
    groups = tile.shape[0] // SUB
    t = tile.astype(jnp.float32)
    out = t[0:SUB]
    for g in range(1, groups):
        out = out + pltpu.roll(t[g * SUB : (g + 1) * SUB], g * LANES // groups, 1)
    return out.astype(jnp.bfloat16)


def untucked(tile, by, gap):
    groups = by // SUB
    t = tile.astype(jnp.float32)
    turned = [t] + [pltpu.roll(t, LANES - g * LANES // groups, 1) for g in range(1, groups)]
    return jnp.concatenate([joined(part, gap) for part in turned], axis=0)


def fetch_kernel(*refs):
    sources, refs = refs[:13], refs[13:]
    tables, scales, tile = refs[:3]
    targets, small, sems = refs[3:7], refs[7:16], refs[16]
    copies = [
        pltpu.make_async_copy(source, target, sems.at[k])
        for k, (source, target) in enumerate(zip(sources, small + targets))
    ]
    for copy in copies:
        copy.start()
    for copy in copies[:9]:
        copy.wait()
    near_rows, near_cols, near_scale, far_rows, far_cols, far_rank, far_scale = small[:7]
    for k, part in enumerate((near_rows, near_cols, far_rows, far_cols, far_rank)):
        tables[k : k + 1, 0 : part.shape[1]] = part[...]
    for k, part in enumerate((near_scale, far_scale)):
        scales[k : k + 1, 0 : part.shape[1]] = part[...]
    d = small[7][...] * small[8][...].astype(jnp.float32)
    by, bx = d.shape
    tile[...] = jnp.concatenate([d, jnp.zeros((by, LANES - bx), jnp.float32)], axis=1)
    for copy in copies[9:]:
        copy.wait()


def blocks_kernel(dims, *refs):
    n_sea, n_fault, n_near, n_far, leaf, rank, rows, leaf_count, bx, wx = dims
    tables, scales, tile = refs[:3]
    refs = refs[3:]
    slots = refs[:n_sea]
    near, left, right, own = refs[n_sea : 4 + n_sea]
    outs = refs[4 + n_sea : 3 + n_sea + n_fault]
    rims = refs[3 + n_sea + n_fault : 2 + n_sea + 2 * n_fault]
    slip, coeffs, acc, wide = refs[2 + n_sea + 2 * n_fault :]
    sea = lax.axis_index("sea")
    fault = lax.axis_index("fault")
    members = slip.shape[1]
    by = tile.shape[0]
    width = leaf_count * leaf // by
    halo = (wx - bx) // 2
    for k in range(n_sea):
        start = pl.multiple_of((sea ^ k) * rows, rows)
        slip[pl.ds(start, rows)] = slots[k][...]
    acc[...] = jnp.zeros_like(acc)
    edge = jnp.zeros((halo,) + wide.shape[1:], jnp.float32)
    wide[0:halo] = edge
    wide[halo + width :] = edge
    level = lax.broadcasted_iota(jnp.int32, (rank, members), 0)
    for b in range(n_far):
        start = pl.multiple_of(tables[3, b] * leaf, leaf)
        c = jnp.dot(
            right[b], slip[pl.ds(start, leaf), :], preferred_element_type=jnp.float32
        )
        coeffs[b] = jnp.where(level < tables[4, b], c, 0.0).astype(jnp.bfloat16)
    for b in range(n_near):
        start = pl.multiple_of(tables[1, b] * leaf, leaf)
        target = pl.multiple_of(tables[0, b] * leaf, leaf)
        term = jnp.dot(
            near[b], slip[pl.ds(start, leaf), :], preferred_element_type=jnp.float32
        )
        acc[pl.ds(target, leaf), :] += scales[0, b] * term
    for b in range(n_far):
        target = pl.multiple_of(tables[2, b] * leaf, leaf)
        term = lax.dot_general(
            left[b], coeffs[b], (((0,), (0,)), ((), ())), preferred_element_type=jnp.float32
        )
        acc[pl.ds(target, leaf), :] += scales[1, b] * term
    wide[halo : halo + width] = jnp.swapaxes(acc[...].reshape(by, width, members), 0, 1)
    own[...] = wide[pl.ds(fault * bx, wx)].reshape(wx * by, members)
    packed = tucked(pieces(tile[...], bx))
    reach = bx + halo
    for k in range(1, n_fault):
        target = fault ^ k
        start = target * bx
        base = start + jnp.where(target == 0, halo, 0)
        part = wide[pl.ds(base, reach)].reshape(reach * by, members)
        outs[k - 1][0 : reach * by] = part.astype(jnp.bfloat16)
        if beside(k):
            outs[k - 1][reach * by :] = packed
        part = wide[pl.ds(start + reach, halo)].reshape(halo * by, members)
        rims[k - 1][...] = part.astype(jnp.bfloat16)


def sum_kernel(dims, *refs):
    n_fault, bx, wx, by = dims
    tile, own = refs[:2]
    parts = refs[2 : 1 + n_fault]
    rims = refs[1 + n_fault : 2 * n_fault]
    total, depth, near_edge, far_edge = refs[2 * n_fault :]
    sea = lax.axis_index("sea")
    fault = lax.axis_index("fault")
    halo = (wx - bx) // 2
    reach = (bx + halo) * by
    main = parts[0][0:reach].astype(jnp.float32)
    for part in parts[1:]:
        main = main + part[0:reach].astype(jnp.float32)
    side = rims[0][...].astype(jnp.float32)
    for rim in rims[1:]:
        side = side + rim[...].astype(jnp.float32)
    zero = jnp.zeros_like(side)
    side = jnp.where(fault == n_fault - 1, zero, side)
    inner = jnp.concatenate([main, side], axis=0)
    first = jnp.concatenate([zero, main], axis=0)
    s = own[...] + jnp.where(fault == 0, first, inner)
    total[...] = s
    mid = tile[...]
    before = jnp.zeros_like(mid)
    after = jnp.zeros_like(mid)
    for k in range(1, n_fault):
        if not beside(k):
            continue
        other = untucked(parts[k - 1][reach:], by, bx)
        source = fault ^ k
        before = before + jnp.where(source == fault - 1, other, 0.0)
        after = after + jnp.where(source == fault + 1, other, 0.0)
    lanes = mid.shape[1]
    lane = lax.broadcasted_iota(jnp.int32, mid.shape, 1)
    d = jnp.where(lane < halo, pltpu.roll(before, lanes - (bx - halo), 1), 0.0)
    d = d + pltpu.roll(mid, halo, 1)
    d = d + pltpu.roll(jnp.where(lane < halo, after, 0.0), halo + bx, 1)
    depth[...] = d
    packed = pieces(d, lanes // 4)
    odd = sea & 1
    stack = s.reshape(wx, by, s.shape[1])
    first = stack[:, 0:SUB, :].reshape(wx * SUB, -1).astype(jnp.bfloat16)
    last = stack[:, by - SUB :, :].reshape(wx * SUB, -1).astype(jnp.bfloat16)
    near_edge[0 : wx * SUB] = jnp.where(odd == 1, first, last)
    far_edge[0 : wx * SUB] = jnp.where(odd == 1, last, first)
    near_edge[wx * SUB :] = packed
    far_edge[wx * SUB :] = packed


def uplift_kernel(dims, total, depth, uplift, wet):
    bx, wx, by = dims
    halo = (wx - bx) // 2
    across = jnp.transpose(jnp.where(depth[...] > 0.0, 1.0, 0.0))[halo : halo + bx]
    for y in range(by):
        wet[y] = jnp.broadcast_to(across[:, y : y + 1], wet.shape[1:])
    for y in range(by):
        uplift[y] = total[pl.ds(halo * by + y, bx, stride=by), :]


def steps_kernel(dims, total, depth, wet, near_edge, far_edge, level, column, rows):
    bx, wx, by = dims
    halo = (wx - bx) // 2
    sea = lax.axis_index("sea")
    odd = sea & 1
    span = by + 2 * SUB
    folds = span // SUB
    edge = wx * SUB
    lanes = depth.shape[1]
    near = near_edge[...].astype(jnp.float32)
    far = far_edge[...].astype(jnp.float32)
    prev = jnp.where(odd == 1, near, far)
    post = jnp.where(odd == 1, far, near)
    prev_d = joined(prev[edge:], lanes // 4)[by - SUB :]
    post_d = joined(post[edge:], lanes // 4)[0:SUB]
    prev_d = jnp.where(sea == 0, 0.0, prev_d)
    post_d = jnp.where(sea == lax.axis_size("sea") - 1, 0.0, post_d)
    d = jnp.concatenate([prev_d, depth[...], post_d], axis=0)
    scale = gravity_step * height_step
    rows[0] = scale * jnp.minimum(d, pltpu.roll(d, lanes - 1, 1))
    rows[1] = scale * jnp.minimum(d, pltpu.roll(d, span - 1, 0))
    folded = [[rows[k, pl.ds(v, SUB, stride=folds), :] for v in range(folds)] for k in range(2)]

    def spread(part, x):
        return [jnp.broadcast_to(f[:, x : x + 1], (SUB, lanes)) for f in part]

    h = []
    for x in range(wx):
        base = x * span
        column[base : base + SUB] = prev[x * SUB : (x + 1) * SUB]
        column[base + SUB : base + SUB + by] = total[x * by : (x + 1) * by]
        column[base + SUB + by : base + span] = post[x * SUB : (x + 1) * SUB]
        h.append([column[pl.ds(base + v, SUB, stride=folds), :] for v in range(folds)])
    de = [spread(folded[0], x) for x in range(wx)]
    dn = [spread(folded[1], x) for x in range(wx)]
    e = [None] * wx
    n = [None] * wx
    for step in range(STEPS):
        before = None
        for x in range(step, wx - 1 - step):
            here = h[x]
            flow = [a - b for a, b in zip(here, h[x + 1])]
            if step:
                flow = [a + b for a, b in zip(e[x], flow)]
            e[x] = flow
            flux = [a * b for a, b in zip(de[x], flow)]
            if before is not None:
                up = here[1:] + [pltpu.roll(here[0], SUB - 1, 0)]
                flow = [a - b for a, b in zip(here, up)]
                if step:
                    flow = [a + b for a, b in zip(n[x], flow)]
                n[x] = flow
                rise = [a * b for a, b in zip(dn[x], flow)]
                down = [pltpu.roll(rise[-1], 1, 0)] + rise[:-1]
                h[x] = [
                    here[v] - (((flux[v] - before[v]) + rise[v]) - down[v])
                    for v in range(folds)
                ]
            before = flux
    for x in range(bx):
        for v in range(folds):
            column[pl.ds(x * span + v, SUB, stride=folds), :] = h[halo + x][v]
    for y in range(by):
        level[y] = wet[y] * column[pl.ds(SUB + y, bx, stride=span), :]


def on_device(
    slip_rate,
    near_blocks,
    near_rows,
    near_cols,
    near_scale,
    far_left,
    far_right,
    far_rows,
    far_cols,
    far_rank,
    far_scale,
    sea_depth,
    wet_mask,
):
    by, bx = sea_depth.shape
    n_sea = lax.axis_size("sea")
    n_fault = lax.axis_size("fault")
    n_near = near_blocks.shape[2]
    n_far, rank, leaf = far_left.shape[2:]
    rows, members = slip_rate.shape
    leaf_count = by * bx * n_fault // leaf
    wx = bx + 2 * STEPS
    f32, bf16 = jnp.float32, jnp.bfloat16

    across = {}
    for k in range(2, n_sea, 2):
        across[k] = swap(slip_rate, "sea", k)
    across[1] = swap(slip_rate, "sea", 1)
    for k in range(2, n_sea, 2):
        across[k + 1] = swap(across[k], "sea", 1)

    vector = pl.BlockSpec(memory_space=pltpu.VMEM)
    scalar = pl.BlockSpec(memory_space=pltpu.SMEM)
    outside = pl.BlockSpec(memory_space=pltpu.HBM)
    short = [near_rows, near_cols, near_scale, far_rows, far_cols, far_rank, far_scale]
    short = [a[0] for a in short] + [sea_depth, wet_mask]
    heavy = [slip_rate, near_blocks[0, 0], far_left[0, 0], far_right[0, 0]]
    moved = sum(a.size * 2 for a in heavy)
    tables, scales, tile, mine, near, left, right = pl.pallas_call(
        fetch_kernel,
        out_shape=[
            jax.ShapeDtypeStruct((SUB, LANES), jnp.int32),
            jax.ShapeDtypeStruct((SUB, LANES), f32),
            jax.ShapeDtypeStruct((by, LANES), f32),
        ]
        + [jax.ShapeDtypeStruct(a.shape, bf16) for a in heavy],
        in_specs=[outside] * 13,
        out_specs=[vector] * 7,
        scratch_shapes=[pltpu.VMEM(a.shape, a.dtype) for a in short]
        + [pltpu.SemaphoreType.DMA((13,))],
        compiler_params=pltpu.CompilerParams(vmem_limit_bytes=4 << 20),
        cost_estimate=pl.CostEstimate(flops=0, bytes_accessed=2 * moved, transcendentals=0),
        name="fetch",
    )(*[pltpu.with_memory_space_constraint(a, pltpu.HBM) for a in short + heavy])
    slots = [mine] + [across[k] for k in range(1, n_sea)]
    cells = wx * by
    dims = (n_sea, n_fault, n_near, n_far, leaf, rank, rows, leaf_count, bx, wx)
    own, *chunks = pl.pallas_call(
        functools.partial(blocks_kernel, dims),
        out_shape=[jax.ShapeDtypeStruct((cells, members), f32)]
        + [
            jax.ShapeDtypeStruct(((bx + STEPS) * by + SUB * beside(k), members), bf16)
            for k in range(1, n_fault)
        ]
        + [jax.ShapeDtypeStruct((STEPS * by, members), bf16)] * (n_fault - 1),
        in_specs=[scalar] * 2 + [vector] * (n_sea + 4),
        out_specs=[vector] * (2 * n_fault - 1),
        scratch_shapes=[
            pltpu.VMEM((n_sea * rows, members), bf16),
            pltpu.VMEM((n_far, rank, members), bf16),
            pltpu.VMEM((leaf_count * leaf, members), f32),
            pltpu.VMEM((n_fault * bx + 2 * STEPS, by, members), f32),
        ],
        compiler_params=pltpu.CompilerParams(vmem_limit_bytes=12 << 20),
        name="blocks",
    )(
        tables,
        scales,
        tile,
        *slots,
        near,
        left,
        right,
    )

    got = []
    for k in range(1, n_fault):
        got.append(swap(chunks[k - 1], "fault", k))
    last = n_fault - 1
    for k in range(1, n_fault):
        hops = []
        for i in range(n_sea):
            for f in range(n_fault):
                j, g = i, f ^ k
                if g in (0, last) and k == last:
                    j, g = i ^ 1, f
                elif g in (0, last) and last < 2 * k:
                    g = last - g
                hops.append((i * n_fault + f, j * n_fault + g))
        got.append(lax.ppermute(chunks[last + k - 1], ("sea", "fault"), hops))

    edge = jax.ShapeDtypeStruct((wx * SUB + by, members), bf16)
    total, depth, near_edge, far_edge = pl.pallas_call(
        functools.partial(sum_kernel, (n_fault, bx, wx, by)),
        out_shape=[
            jax.ShapeDtypeStruct((cells, members), f32),
            jax.ShapeDtypeStruct((by, members), f32),
            edge,
            edge,
        ],
        in_specs=[vector] * (2 * n_fault),
        out_specs=[vector] * 4,
        compiler_params=pltpu.CompilerParams(vmem_limit_bytes=8 << 20),
        name="sums",
    )(tile, own, *got)

    ring = []
    for i in range(n_sea):
        j = i + 2 * (i & 1) - 1
        for f in range(n_fault):
            inside = 0 <= j < n_sea
            ring.append((i * n_fault + f, j * n_fault + f if inside else i * n_fault + (f ^ 1)))
    far_edge = lax.ppermute(far_edge, ("sea", "fault"), ring)
    near_edge = swap(near_edge, "sea", 1)

    uplift, wet = pl.pallas_call(
        functools.partial(uplift_kernel, (bx, wx, by)),
        out_shape=[jax.ShapeDtypeStruct((by, bx, members), f32)] * 2,
        in_specs=[vector] * 2,
        out_specs=[vector] * 2,
        compiler_params=pltpu.CompilerParams(vmem_limit_bytes=4 << 20),
        cost_estimate=pl.CostEstimate(flops=0, bytes_accessed=16 * cells * members, transcendentals=0),
        name="uplift",
    )(total, depth)
    span = by + 2 * SUB
    level = pl.pallas_call(
        functools.partial(steps_kernel, (bx, wx, by)),
        out_shape=jax.ShapeDtypeStruct((by, bx, members), f32),
        in_specs=[vector] * 5,
        out_specs=vector,
        scratch_shapes=[pltpu.VMEM((wx * span, members), f32), pltpu.VMEM((2, span, LANES), f32)],
        compiler_params=pltpu.CompilerParams(vmem_limit_bytes=8 << 20),
        name="steps",
    )(total, depth, wet, near_edge, far_edge)
    return uplift, level


def solution(mesh):
    placed = (
        P(("fault", "sea"), None),
        P("sea", "fault", None, None, None),
        P("sea", "fault", None),
        P("sea", "fault", None),
        P("sea", "fault", None),
        P("sea", "fault", None, None, None),
        P("sea", "fault", None, None, None),
        P("sea", "fault", None),
        P("sea", "fault", None),
        P("sea", "fault", None),
        P("sea", "fault", None),
        P("sea", "fault"),
        P("sea", "fault"),
    )

    return jax.shard_map(
        on_device,
        mesh=mesh,
        in_specs=placed,
        out_specs=(P("sea", "fault", None), P("sea", "fault", None)),
        check_vma=False,
    )
```

```python
import functools

import jax
import jax.numpy as jnp
from jax import lax
from jax.experimental import pallas as pl
from jax.experimental.pallas import tpu as pltpu
from jax.sharding import PartitionSpec as P


STEPS = 6
SUB = 8
LANES = 128

gravity_step = 0.7
height_step = 0.7


def swap(x, axis, k):
    count = lax.axis_size(axis)
    return lax.ppermute(x, axis, [(i, i ^ k) for i in range(count)])


def pieces(d, gap):
    hi = d.astype(jnp.bfloat16).astype(jnp.float32)
    rest = d - hi
    mid = rest.astype(jnp.bfloat16).astype(jnp.float32)
    low = rest - mid
    packed = hi + pltpu.roll(mid, gap, 1) + pltpu.roll(low, 2 * gap, 1)
    return packed.astype(jnp.bfloat16)


def joined(tile, gap):
    t = tile.astype(jnp.float32)
    lanes = t.shape[1]
    d = (t + pltpu.roll(t, lanes - gap, 1)) + pltpu.roll(t, lanes - 2 * gap, 1)
    lane = lax.broadcasted_iota(jnp.int32, t.shape, 1)
    return jnp.where(lane < gap, d, 0.0)


def beside(k):
    return k & (k + 1) == 0


def tucked(tile):
    groups = tile.shape[0] // SUB
    t = tile.astype(jnp.float32)
    out = t[0:SUB]
    for g in range(1, groups):
        out = out + pltpu.roll(t[g * SUB : (g + 1) * SUB], g * LANES // groups, 1)
    return out.astype(jnp.bfloat16)


def untucked(tile, by, gap):
    groups = by // SUB
    t = tile.astype(jnp.float32)
    turned = [t] + [pltpu.roll(t, LANES - g * LANES // groups, 1) for g in range(1, groups)]
    return jnp.concatenate([joined(part, gap) for part in turned], axis=0)


def fetch_kernel(*refs):
    sources, refs = refs[:13], refs[13:]
    tables, scales, tile = refs[:3]
    targets, small, sems = refs[3:7], refs[7:16], refs[16]
    copies = [
        pltpu.make_async_copy(source, target, sems.at[k])
        for k, (source, target) in enumerate(zip(sources, small + targets))
    ]
    for copy in copies:
        copy.start()
    for copy in copies[:9]:
        copy.wait()
    near_rows, near_cols, near_scale, far_rows, far_cols, far_rank, far_scale = small[:7]
    for k, part in enumerate((near_rows, near_cols, far_rows, far_cols, far_rank)):
        tables[k : k + 1, 0 : part.shape[1]] = part[...]
    for k, part in enumerate((near_scale, far_scale)):
        scales[k : k + 1, 0 : part.shape[1]] = part[...]
    d = small[7][...] * small[8][...].astype(jnp.float32)
    by, bx = d.shape
    tile[...] = jnp.concatenate([d, jnp.zeros((by, LANES - bx), jnp.float32)], axis=1)
    for copy in copies[9:]:
        copy.wait()


def blocks_kernel(dims, *refs):
    n_sea, n_fault, n_near, n_far, leaf, rank, rows, leaf_count, bx, wx = dims
    tables, scales, tile = refs[:3]
    refs = refs[3:]
    slots = refs[:n_sea]
    near, left, right, own = refs[n_sea : 4 + n_sea]
    outs = refs[4 + n_sea : 3 + n_sea + n_fault]
    rims = refs[3 + n_sea + n_fault : 2 + n_sea + 2 * n_fault]
    slip, coeffs, acc, wide = refs[2 + n_sea + 2 * n_fault :]
    sea = lax.axis_index("sea")
    fault = lax.axis_index("fault")
    members = slip.shape[1]
    by = tile.shape[0]
    width = leaf_count * leaf // by
    halo = (wx - bx) // 2
    for k in range(n_sea):
        start = pl.multiple_of((sea ^ k) * rows, rows)
        slip[pl.ds(start, rows)] = slots[k][...]
    acc[...] = jnp.zeros_like(acc)
    edge = jnp.zeros((halo,) + wide.shape[1:], jnp.float32)
    wide[0:halo] = edge
    wide[halo + width :] = edge
    level = lax.broadcasted_iota(jnp.int32, (rank, members), 0)
    for b in range(n_far):
        start = pl.multiple_of(tables[3, b] * leaf, leaf)
        c = jnp.dot(
            right[b], slip[pl.ds(start, leaf), :], preferred_element_type=jnp.float32
        )
        coeffs[b] = jnp.where(level < tables[4, b], c, 0.0).astype(jnp.bfloat16)
    for b in range(n_near):
        start = pl.multiple_of(tables[1, b] * leaf, leaf)
        target = pl.multiple_of(tables[0, b] * leaf, leaf)
        term = jnp.dot(
            near[b], slip[pl.ds(start, leaf), :], preferred_element_type=jnp.float32
        )
        acc[pl.ds(target, leaf), :] += scales[0, b] * term
    for b in range(n_far):
        target = pl.multiple_of(tables[2, b] * leaf, leaf)
        term = lax.dot_general(
            left[b], coeffs[b], (((0,), (0,)), ((), ())), preferred_element_type=jnp.float32
        )
        acc[pl.ds(target, leaf), :] += scales[1, b] * term
    wide[halo : halo + width] = jnp.swapaxes(acc[...].reshape(by, width, members), 0, 1)
    own[...] = wide[pl.ds(fault * bx, wx)].reshape(wx * by, members)
    packed = tucked(pieces(tile[...], bx))
    reach = bx + halo
    for k in range(1, n_fault):
        target = fault ^ k
        start = target * bx
        base = start + jnp.where(target == 0, halo, 0)
        part = wide[pl.ds(base, reach)].reshape(reach * by, members)
        outs[k - 1][0 : reach * by] = part.astype(jnp.bfloat16)
        if beside(k):
            outs[k - 1][reach * by :] = packed
        part = wide[pl.ds(start + reach, halo)].reshape(halo * by, members)
        rims[k - 1][...] = part.astype(jnp.bfloat16)


def sum_kernel(dims, *refs):
    n_fault, bx, wx, by = dims
    tile, own = refs[:2]
    parts = refs[2 : 1 + n_fault]
    rims = refs[1 + n_fault : 2 * n_fault]
    total, depth, near_edge, far_edge = refs[2 * n_fault :]
    sea = lax.axis_index("sea")
    fault = lax.axis_index("fault")
    halo = (wx - bx) // 2
    reach = (bx + halo) * by
    main = parts[0][0:reach].astype(jnp.float32)
    for part in parts[1:]:
        main = main + part[0:reach].astype(jnp.float32)
    side = rims[0][...].astype(jnp.float32)
    for rim in rims[1:]:
        side = side + rim[...].astype(jnp.float32)
    zero = jnp.zeros_like(side)
    side = jnp.where(fault == n_fault - 1, zero, side)
    inner = jnp.concatenate([main, side], axis=0)
    first = jnp.concatenate([zero, main], axis=0)
    s = own[...] + jnp.where(fault == 0, first, inner)
    total[...] = s
    mid = tile[...]
    before = jnp.zeros_like(mid)
    after = jnp.zeros_like(mid)
    for k in range(1, n_fault):
        if not beside(k):
            continue
        other = untucked(parts[k - 1][reach:], by, bx)
        source = fault ^ k
        before = before + jnp.where(source == fault - 1, other, 0.0)
        after = after + jnp.where(source == fault + 1, other, 0.0)
    lanes = mid.shape[1]
    lane = lax.broadcasted_iota(jnp.int32, mid.shape, 1)
    d = jnp.where(lane < halo, pltpu.roll(before, lanes - (bx - halo), 1), 0.0)
    d = d + pltpu.roll(mid, halo, 1)
    d = d + pltpu.roll(jnp.where(lane < halo, after, 0.0), halo + bx, 1)
    depth[...] = d
    packed = pieces(d, lanes // 4)
    odd = sea & 1
    stack = s.reshape(wx, by, s.shape[1])
    first = stack[:, 0:SUB, :].reshape(wx * SUB, -1).astype(jnp.bfloat16)
    last = stack[:, by - SUB :, :].reshape(wx * SUB, -1).astype(jnp.bfloat16)
    near_edge[0 : wx * SUB] = jnp.where(odd == 1, first, last)
    far_edge[0 : wx * SUB] = jnp.where(odd == 1, last, first)
    near_edge[wx * SUB :] = packed
    far_edge[wx * SUB :] = packed


def uplift_kernel(dims, total, depth, uplift, wet):
    bx, wx, by = dims
    halo = (wx - bx) // 2
    across = jnp.transpose(jnp.where(depth[...] > 0.0, 1.0, 0.0))[halo : halo + bx]
    for y in range(by):
        wet[y] = jnp.broadcast_to(across[:, y : y + 1], wet.shape[1:])
    for y in range(by):
        uplift[y] = total[pl.ds(halo * by + y, bx, stride=by), :]


def steps_kernel(dims, total, depth, wet, near_edge, far_edge, level, column, rows):
    bx, wx, by = dims
    halo = (wx - bx) // 2
    sea = lax.axis_index("sea")
    odd = sea & 1
    span = by + 2 * SUB
    folds = span // SUB
    edge = wx * SUB
    lanes = depth.shape[1]
    near = near_edge[...].astype(jnp.float32)
    far = far_edge[...].astype(jnp.float32)
    prev = jnp.where(odd == 1, near, far)
    post = jnp.where(odd == 1, far, near)
    prev_d = joined(prev[edge:], lanes // 4)[by - SUB :]
    post_d = joined(post[edge:], lanes // 4)[0:SUB]
    prev_d = jnp.where(sea == 0, 0.0, prev_d)
    post_d = jnp.where(sea == lax.axis_size("sea") - 1, 0.0, post_d)
    d = jnp.concatenate([prev_d, depth[...], post_d], axis=0)
    scale = gravity_step * height_step
    rows[...] = scale * d
    folded = [rows[pl.ds(v, SUB, stride=folds), :] for v in range(folds)]

    cell = [
        [jnp.broadcast_to(f[:, x : x + 1], (SUB, lanes)) for f in folded] for x in range(wx)
    ]
    de = [[jnp.minimum(a, b) for a, b in zip(cell[x], cell[x + 1])] for x in range(wx - 1)]
    dn = [
        [jnp.minimum(a, b) for a, b in zip(c, c[1:] + [pltpu.roll(c[0], SUB - 1, 0)])]
        for c in cell
    ]
    h = []
    for x in range(wx):
        base = x * span
        column[base : base + SUB] = prev[x * SUB : (x + 1) * SUB]
        column[base + SUB : base + SUB + by] = total[x * by : (x + 1) * by]
        column[base + SUB + by : base + span] = post[x * SUB : (x + 1) * SUB]
        h.append([column[pl.ds(base + v, SUB, stride=folds), :] for v in range(folds)])
    e = [None] * wx
    n = [None] * wx
    for step in range(STEPS):
        before = None
        for x in range(step, wx - 1 - step):
            here = h[x]
            flow = [a - b for a, b in zip(here, h[x + 1])]
            if step:
                flow = [a + b for a, b in zip(e[x], flow)]
            e[x] = flow
            flux = [a * b for a, b in zip(de[x], flow)]
            if before is not None:
                up = here[1:] + [pltpu.roll(here[0], SUB - 1, 0)]
                flow = [a - b for a, b in zip(here, up)]
                if step:
                    flow = [a + b for a, b in zip(n[x], flow)]
                n[x] = flow
                rise = [a * b for a, b in zip(dn[x], flow)]
                down = [pltpu.roll(rise[-1], 1, 0)] + rise[:-1]
                h[x] = [
                    here[v] - (((flux[v] - before[v]) + rise[v]) - down[v])
                    for v in range(folds)
                ]
            before = flux
    for x in range(bx):
        for v in range(folds):
            column[pl.ds(x * span + v, SUB, stride=folds), :] = h[halo + x][v]
    for y in range(by):
        level[y] = wet[y] * column[pl.ds(SUB + y, bx, stride=span), :]


def on_device(
    slip_rate,
    near_blocks,
    near_rows,
    near_cols,
    near_scale,
    far_left,
    far_right,
    far_rows,
    far_cols,
    far_rank,
    far_scale,
    sea_depth,
    wet_mask,
):
    by, bx = sea_depth.shape
    n_sea = lax.axis_size("sea")
    n_fault = lax.axis_size("fault")
    n_near = near_blocks.shape[2]
    n_far, rank, leaf = far_left.shape[2:]
    rows, members = slip_rate.shape
    leaf_count = by * bx * n_fault // leaf
    wx = bx + 2 * STEPS
    f32, bf16 = jnp.float32, jnp.bfloat16

    across = {}
    for k in range(2, n_sea, 2):
        across[k] = swap(slip_rate, "sea", k)
    across[1] = swap(slip_rate, "sea", 1)
    for k in range(2, n_sea, 2):
        across[k + 1] = swap(across[k], "sea", 1)

    vector = pl.BlockSpec(memory_space=pltpu.VMEM)
    scalar = pl.BlockSpec(memory_space=pltpu.SMEM)
    outside = pl.BlockSpec(memory_space=pltpu.HBM)
    short = [near_rows, near_cols, near_scale, far_rows, far_cols, far_rank, far_scale]
    short = [a[0] for a in short] + [sea_depth, wet_mask]
    heavy = [slip_rate, near_blocks[0, 0], far_left[0, 0], far_right[0, 0]]
    moved = sum(a.size * 2 for a in heavy)
    tables, scales, tile, mine, near, left, right = pl.pallas_call(
        fetch_kernel,
        out_shape=[
            jax.ShapeDtypeStruct((SUB, LANES), jnp.int32),
            jax.ShapeDtypeStruct((SUB, LANES), f32),
            jax.ShapeDtypeStruct((by, LANES), f32),
        ]
        + [jax.ShapeDtypeStruct(a.shape, bf16) for a in heavy],
        in_specs=[outside] * 13,
        out_specs=[vector] * 7,
        scratch_shapes=[pltpu.VMEM(a.shape, a.dtype) for a in short]
        + [pltpu.SemaphoreType.DMA((13,))],
        compiler_params=pltpu.CompilerParams(vmem_limit_bytes=4 << 20),
        cost_estimate=pl.CostEstimate(flops=0, bytes_accessed=2 * moved, transcendentals=0),
        name="fetch",
    )(*[pltpu.with_memory_space_constraint(a, pltpu.HBM) for a in short + heavy])
    slots = [mine] + [across[k] for k in range(1, n_sea)]
    cells = wx * by
    dims = (n_sea, n_fault, n_near, n_far, leaf, rank, rows, leaf_count, bx, wx)
    own, *chunks = pl.pallas_call(
        functools.partial(blocks_kernel, dims),
        out_shape=[jax.ShapeDtypeStruct((cells, members), f32)]
        + [
            jax.ShapeDtypeStruct(((bx + STEPS) * by + SUB * beside(k), members), bf16)
            for k in range(1, n_fault)
        ]
        + [jax.ShapeDtypeStruct((STEPS * by, members), bf16)] * (n_fault - 1),
        in_specs=[scalar] * 2 + [vector] * (n_sea + 4),
        out_specs=[vector] * (2 * n_fault - 1),
        scratch_shapes=[
            pltpu.VMEM((n_sea * rows, members), bf16),
            pltpu.VMEM((n_far, rank, members), bf16),
            pltpu.VMEM((leaf_count * leaf, members), f32),
            pltpu.VMEM((n_fault * bx + 2 * STEPS, by, members), f32),
        ],
        compiler_params=pltpu.CompilerParams(vmem_limit_bytes=12 << 20),
        name="blocks",
    )(
        tables,
        scales,
        tile,
        *slots,
        near,
        left,
        right,
    )

    got = []
    for k in range(1, n_fault):
        got.append(swap(chunks[k - 1], "fault", k))
    last = n_fault - 1
    for k in range(1, n_fault):
        hops = []
        for i in range(n_sea):
            for f in range(n_fault):
                j, g = i, f ^ k
                if g in (0, last) and k == last:
                    j, g = i ^ 1, f
                elif g in (0, last) and last < 2 * k:
                    g = last - g
                hops.append((i * n_fault + f, j * n_fault + g))
        got.append(lax.ppermute(chunks[last + k - 1], ("sea", "fault"), hops))

    edge = jax.ShapeDtypeStruct((wx * SUB + by, members), bf16)
    total, depth, near_edge, far_edge = pl.pallas_call(
        functools.partial(sum_kernel, (n_fault, bx, wx, by)),
        out_shape=[
            jax.ShapeDtypeStruct((cells, members), f32),
            jax.ShapeDtypeStruct((by, members), f32),
            edge,
            edge,
        ],
        in_specs=[vector] * (2 * n_fault),
        out_specs=[vector] * 4,
        compiler_params=pltpu.CompilerParams(vmem_limit_bytes=8 << 20),
        name="sums",
    )(tile, own, *got)

    ring = []
    for i in range(n_sea):
        j = i + 2 * (i & 1) - 1
        for f in range(n_fault):
            inside = 0 <= j < n_sea
            ring.append((i * n_fault + f, j * n_fault + f if inside else i * n_fault + (f ^ 1)))
    far_edge = lax.ppermute(far_edge, ("sea", "fault"), ring)
    near_edge = swap(near_edge, "sea", 1)

    uplift, wet = pl.pallas_call(
        functools.partial(uplift_kernel, (bx, wx, by)),
        out_shape=[jax.ShapeDtypeStruct((by, bx, members), f32)] * 2,
        in_specs=[vector] * 2,
        out_specs=[vector] * 2,
        compiler_params=pltpu.CompilerParams(vmem_limit_bytes=4 << 20),
        cost_estimate=pl.CostEstimate(flops=0, bytes_accessed=16 * cells * members, transcendentals=0),
        name="uplift",
    )(total, depth)
    span = by + 2 * SUB
    level = pl.pallas_call(
        functools.partial(steps_kernel, (bx, wx, by)),
        out_shape=jax.ShapeDtypeStruct((by, bx, members), f32),
        in_specs=[vector] * 5,
        out_specs=vector,
        scratch_shapes=[pltpu.VMEM((wx * span, members), f32), pltpu.VMEM((span, LANES), f32)],
        compiler_params=pltpu.CompilerParams(vmem_limit_bytes=8 << 20),
        name="steps",
    )(total, depth, wet, near_edge, far_edge)
    return uplift, level


def solution(mesh):
    placed = (
        P(("fault", "sea"), None),
        P("sea", "fault", None, None, None),
        P("sea", "fault", None),
        P("sea", "fault", None),
        P("sea", "fault", None),
        P("sea", "fault", None, None, None),
        P("sea", "fault", None, None, None),
        P("sea", "fault", None),
        P("sea", "fault", None),
        P("sea", "fault", None),
        P("sea", "fault", None),
        P("sea", "fault"),
        P("sea", "fault"),
    )

    return jax.shard_map(
        on_device,
        mesh=mesh,
        in_specs=placed,
        out_specs=(P("sea", "fault", None), P("sea", "fault", None)),
        check_vma=False,
    )
```
